128 devices in a mesh: dp: 8 (over z, y_hi), head: 16 (over y_lo, x, core).
Axes of the slice: x: 4, y: 4 (y_hi: 2, y_lo: 2; y = y_hi * 2 + y_lo), z: 4, core: 2. Of those that a mesh axis runs over, the one named last changes fastest.
Arguments:
- ckpt_query: bfloat16 [4, 8192, 8192], P(None, ('dp', 'head')), may hold values from -0.125 to 0.125
- ckpt_key: bfloat16 [4, 8192, 1024], P(None, ('dp', 'head')), may hold values from -0.125 to 0.125
- ckpt_value: bfloat16 [4, 8192, 1024], P(None, ('dp', 'head')), may hold values from -0.125 to 0.125
- ckpt_output: bfloat16 [4, 8192, 8192], P(None, ('head', 'dp')), may hold values from -0.125 to 0.125
- hidden_in: bfloat16 [4096, 8192], P('dp'), may hold values from -17 to 17
- segment_ids: int32 [8, 512], P('dp'), may hold values from 0 to 3, never falling along the last dimension, each value on 1 to 256 neighbouring positions
Outputs:
- attn_out: bfloat16 [4096, 8192], P('dp', 'head')
The draws below stay inside these ranges and needn't reach their ends.
All inputs are finite; a program needn't handle non-finite values.
Results may differ from the reference program's by a relative error of at most 0.01.
The reference program's roundings to bfloat16 on the way (of `mean_query`, `q_rot`, `probs` and `context`) count: a program that leaves them out, or rounds other values in their place, can miss the bound.
Values may be sent and summed in bfloat16 or wider, within the bound.
A program may use at most 128 MiB of HBM per device.

```python
import math
import jax
import jax.numpy as jnp
import numpy as np
from jax import lax

D = 8192
HEADS = 64
KV = 8
HD = 128
CKPTS = 4
TOK_DEV = 512
QW = 8192
KVW = 1024
TOKENS = 4096
N_DP = 8


def draw_hidden_in(key, part):
    first_key = jax.random.fold_in(key, 0)
    base = jnp.clip(jax.random.normal(first_key, (TOKENS, D), jnp.float32), -8.0, 8.0)
    return base.astype(jnp.bfloat16)


def block_levels(rng, shape, shards, low, high):
    factor_of = 1.0
    for axis_at, shards_of in shards:
        heights = jax.random.uniform(jax.random.fold_in(jax.random.fold_in(rng, 6), axis_at), (shards_of,), jnp.float32, low / len(shards), high / len(shards))
        factor_of = factor_of * jnp.repeat(jnp.exp(heights), shape[axis_at] // shards_of).reshape((-1,) + (1,) * (len(shape) - 1 - axis_at))
    return factor_of


def profile(count, total, limit, lean):
    portions = [(1 << 20) // math.isqrt(rank ** lean) + 1 for rank in range(2, count + 1)]
    rest, counts = total - limit - (count - 1), [1] * (count - 1)
    while rest > 0:
        free = [i for i in range(count - 1) if counts[i] < limit]
        pool, remaining = sum([portions[i] for i in free]), rest
        for i in free:
            more = min(limit - counts[i], max(1, remaining * portions[i] // pool), rest)
            counts[i] = counts[i] + more
            rest = rest - more
    return np.array([limit] + counts)


def uneven_parts(own_key, number_of, total, most, slope):
    if number_of == 2:
        one = jax.random.randint(own_key, (), max(1, total - most), min(most, total - 1) + 1)
        return jnp.stack([one, total - one])
    tallies = jnp.asarray(profile(number_of, total, most, slope), jnp.int32)
    couples = (number_of - 1) // 2
    giver, sink = tallies[1:1 + 2 * couples:2], tallies[2:2 + 2 * couples:2]
    slack = jnp.minimum(giver - 1, most - sink)
    moved = jax.random.randint(jax.random.fold_in(own_key, 1), (couples,), 0, 1 << 20) % (slack + 1)
    tallies = tallies.at[1:1 + 2 * couples:2].set(giver - moved).at[2:2 + 2 * couples:2].set(sink + moved)
    return tallies[jax.random.permutation(jax.random.fold_in(own_key, 2), number_of)]


def centred(stream_key, dims, scale, limit, shards=(), held_as=jnp.bfloat16):
    values = scale * jax.random.normal(stream_key, dims, jnp.float32)
    if shards:
        values = values * block_levels(stream_key, dims, shards, -0.22, 0.18)
    return jnp.clip(values, -limit, limit).astype(held_as)


def setup_inputs(seed: int = 0) -> dict:
    streams_of = jax.random.split(jax.random.key(seed), 7)
    ckpt_query = centred(streams_of[0], (CKPTS, D, QW), (D // 4) ** -0.5, 0.125, ((1, 128),))
    ckpt_key = centred(streams_of[1], (CKPTS, D, KVW), (D // 4) ** -0.5, 0.125, ((1, 128),))
    ckpt_value = centred(streams_of[2], (CKPTS, D, KVW), (D // 4) ** -0.5, 0.125, ((1, 128),))
    ckpt_output = centred(streams_of[3], (CKPTS, D, QW), (QW // 4) ** -0.5, 0.125, ((1, 128),))
    hidden_in = draw_hidden_in(jax.random.fold_in(streams_of[6], 71), 0)
    segment_ids = jax.vmap(lambda own: jnp.searchsorted(jnp.cumsum(uneven_parts(own, 4, TOK_DEV, TOK_DEV // 2, 0)), jnp.arange(TOK_DEV), side="right"))(jax.random.split(streams_of[5], N_DP)).reshape((N_DP, TOK_DEV)).astype(jnp.int32)
    return {"ckpt_query": ckpt_query, "ckpt_key": ckpt_key, "ckpt_value": ckpt_value, "ckpt_output": ckpt_output, "hidden_in": hidden_in, "segment_ids": segment_ids}


rope_base = 500000.0


def average(stack):
    return (jnp.sum(stack.astype(jnp.float32), axis=0) * 0.25).astype(jnp.bfloat16)


def rotate(values, positions):
    half = values.shape[-1] // 2
    freq = rope_base ** (-2.0 * jnp.arange(half, dtype=jnp.float32) / values.shape[-1])
    angle = positions[:, None] * freq[None, :]
    cosine = jnp.cos(angle)[:, None, :]
    sine = jnp.sin(angle)[:, None, :]
    first = values[..., :half]
    second = values[..., half:]
    return jnp.concatenate([first * cosine - second * sine, second * cosine + first * sine], axis=-1)


def reference(ckpt_query, ckpt_key, ckpt_value, ckpt_output, hidden_in, segment_ids):
    mean_query = average(ckpt_query)
    mean_key = average(ckpt_key)
    mean_value = average(ckpt_value)
    mean_output = average(ckpt_output)
    query = jnp.dot(hidden_in, mean_query, preferred_element_type=jnp.float32)
    keys = jnp.dot(hidden_in, mean_key, preferred_element_type=jnp.float32)
    values = jnp.dot(hidden_in, mean_value, preferred_element_type=jnp.float32)
    rows = segment_ids.shape[0]
    tok = hidden_in.shape[0] // rows
    positions = jnp.arange(tok, dtype=jnp.float32)
    q_rot = rotate(query.reshape(rows, tok, HEADS, HD), positions).astype(jnp.bfloat16)
    k_rot = rotate(keys.reshape(rows, tok, KV, HD), positions).astype(jnp.bfloat16)
    v_b = values.reshape(rows, tok, KV, HD).astype(jnp.bfloat16)
    order = jnp.arange(tok, dtype=jnp.int32)

    def one_row(inputs):
        q_row, k_row, v_row, seg = inputs
        key_all = jnp.repeat(k_row, HEADS // KV, axis=1).astype(jnp.float32)
        value_all = jnp.repeat(v_row, HEADS // KV, axis=1).astype(jnp.float32)
        scores = jnp.einsum("qhd,khd->hqk", q_row.astype(jnp.float32), key_all) * (HD ** -0.5)
        allowed = (order[:, None] >= order[None, :]) & (seg[:, None] == seg[None, :])
        scores = jnp.where(allowed[None], scores, -1e30)
        peak = jnp.max(scores, axis=-1, keepdims=True)
        weights = jnp.exp(scores - peak)
        probs = (weights / jnp.sum(weights, axis=-1, keepdims=True)).astype(jnp.bfloat16)
        context = jnp.einsum("hqk,khd->qhd", probs.astype(jnp.float32), value_all)
        return context.astype(jnp.bfloat16).reshape(tok, HEADS * HD)

    context = lax.map(one_row, (q_rot, k_rot, v_b, segment_ids)).reshape(rows * tok, HEADS * HD)
    result = lax.dot_general(context, mean_output, (((1,), (1,)), ((), ())), preferred_element_type=jnp.float32)
    return result.astype(jnp.bfloat16)
```

```python
import jax
import jax.numpy as jnp
from jax import lax
from jax.sharding import PartitionSpec as P

rope_base = 500000.0


def average(stack):
    return (jnp.sum(stack.astype(jnp.float32), axis=0) * 0.25).astype(jnp.bfloat16)


def rotate(values, positions):
    half = values.shape[-1] // 2
    freq = rope_base ** (-2.0 * jnp.arange(half, dtype=jnp.float32) / values.shape[-1])
    angle = positions[:, None] * freq[None, :]
    cosine = jnp.cos(angle)[:, None, :]
    sine = jnp.sin(angle)[:, None, :]
    first = values[..., :half]
    second = values[..., half:]
    return jnp.concatenate(
        [first * cosine - second * sine, second * cosine + first * sine], axis=-1
    )


def shards(ckpt_query, ckpt_key, ckpt_value, ckpt_output, hidden_in, segment_ids):
    n_dp = lax.axis_size("dp")
    n_head = lax.axis_size("head")
    rows, wide = ckpt_query.shape[1:]
    kv_wide = ckpt_key.shape[2]
    output_rows = lax.all_gather(average(ckpt_output), "dp", axis=0, tiled=True)
    mean_query = average(ckpt_query).reshape(rows, n_head, wide // n_head)
    mean_key = average(ckpt_key).reshape(rows, n_head, kv_wide // n_head)
    mean_value = average(ckpt_value).reshape(rows, n_head, kv_wide // n_head)
    packed = jnp.concatenate([mean_query, mean_key, mean_value], axis=2).transpose(1, 0, 2)
    moved = lax.all_to_all(packed, "head", split_axis=0, concat_axis=0, tiled=True)
    gathered = lax.all_gather(moved.reshape(n_head * rows, -1), "dp", axis=0, tiled=True)
    tok = hidden_in.shape[0]
    projected = jnp.dot(hidden_in, gathered, preferred_element_type=jnp.float32)
    query = projected[:, : wide // n_head]
    head_size = 2 * kv_wide // n_head
    own = projected[:, wide // n_head :]
    position = lax.axis_index("head")
    other = lax.ppermute(own, "head", [(i, i ^ 1) for i in range(n_head)])
    half = head_size // 2
    lower = position % 2 == 0
    low = jnp.where(lower, own, other)
    high = jnp.where(lower, other, own)
    keys = jnp.concatenate([low[:, :half], high[:, :half]], axis=1)
    values = jnp.concatenate([low[:, half:], high[:, half:]], axis=1)
    heads_here = query.shape[1] // head_size
    positions = jnp.arange(tok, dtype=jnp.float32)
    q_rot = rotate(query.reshape(tok, heads_here, head_size), positions).astype(jnp.bfloat16)
    k_rot = rotate(keys.reshape(tok, 1, head_size), positions)[:, 0].astype(jnp.bfloat16)
    v_b = values.astype(jnp.bfloat16)
    scores = jnp.einsum(
        "qhd,kd->hqk", q_rot, k_rot, preferred_element_type=jnp.float32
    ) * head_size ** (-0.5)
    order = jnp.arange(tok, dtype=jnp.int32)
    segment = segment_ids[0]
    allowed = (order[:, None] >= order[None, :]) & (segment[:, None] == segment[None, :])
    scores = jnp.where(allowed[None], scores, -1e30)
    peak = jnp.max(scores, axis=-1, keepdims=True)
    weights = jnp.exp(scores - peak)
    probs = (weights / jnp.sum(weights, axis=-1, keepdims=True)).astype(jnp.bfloat16)
    context = jnp.einsum("hqk,kd->qhd", probs, v_b, preferred_element_type=jnp.float32)
    context = context.astype(jnp.bfloat16).reshape(tok, heads_here * head_size)
    everyone = lax.all_gather(context, "head", axis=0)
    weight = output_rows.reshape(output_rows.shape[0], n_head, wide // n_head)
    result = lax.dot_general(
        everyone,
        weight,
        (((0, 2), (1, 2)), ((), ())),
        preferred_element_type=jnp.float32,
    )
    return result.astype(jnp.bfloat16)


def solution(mesh):
    placed = (
        P(None, ("dp", "head"), None),
        P(None, ("dp", "head"), None),
        P(None, ("dp", "head"), None),
        P(None, ("head", "dp"), None),
        P("dp", None),
        P("dp", None),
    )
    return jax.shard_map(
        shards, mesh=mesh, in_specs=placed, out_specs=P("dp", "head"), check_vma=False
    )
```

```python
import functools

import jax
import jax.numpy as jnp
import numpy as np
from jax import lax
from jax.experimental import pallas as pl
from jax.experimental.pallas import tpu as pltpu
from jax.sharding import PartitionSpec as P

MESH = pl.DeviceIdType.MESH
rope_base = 500000.0
N = 4
TOK = 512
HEAD = 128
HEADS_CHIP = 4
QCOLS = HEADS_CHIP * HEAD
WCOLS = QCOLS + HEAD
ROWS = 64
D = 8192
SUB = 4
PIECE = D // N


def average(stack):
    return (jnp.sum(stack.astype(jnp.float32), axis=0) * 0.25).astype(jnp.bfloat16)


def wrap(value):
    return lax.rem(value, N)


def device(x, y, z, c):
    return (2 * z + lax.div(y, 2), 8 * lax.rem(y, 2) + 2 * x + c)


def kernel(
    ckpt_q, ckpt_k, ckpt_v, ckpt_o, hidden, segments, cosine, sine, out,
    stage_q, stage_kv, stage_o, mean_kv, send_w, send_o, weights, hid, acc, weights_o,
    ctx, q_rot, kv, seg, table, out_block,
    stage_q_sem, stage_sem, a2a_send, a2a_recv, z_send, z_recv, pair_send, pair_recv,
    hid_sem, cross_send, cross_recv, ring_send, ring_recv, kv_sem, seg_sem,
    swap_sem, zo_send, zo_recv, pair_o_send, pair_o_recv, ctx_send, ctx_recv, out_sem,
):
    dp = lax.axis_index("dp")
    head = lax.axis_index("head")
    z = lax.div(dp, 2)
    y_hi = lax.rem(dp, 2)
    y = 2 * y_hi + lax.div(head, 8)
    x = wrap(lax.div(head, 2))
    c = lax.rem(head, 2)
    place = 4 * y + x
    owner = c == y_hi
    up, down, far = wrap(z + 1), wrap(z + 3), wrap(z + 2)
    here_up, here_down = device(x, y, up, c), device(x, y, down, c)
    partner = device(x, y, z, 1 - c)
    across = device(x, wrap(y + 2), z, 1 - c)
    cross = device(x, 3 - y, z, c)

    def remote(src, dst, send, recv, where):
        return pltpu.make_async_remote_copy(
            src_ref=src, dst_ref=dst, send_sem=send, recv_sem=recv,
            device_id=where, device_id_type=MESH,
        )

    def spot(k):
        dx, dy = lax.rem(k, N), lax.div(k, N)
        tx, ty = wrap(x + dx), wrap(y + dy)
        fx, fy = wrap(x + N - dx), wrap(y + N - dy)
        return tx, ty, 4 * ty + tx, 4 * fy + fx

    def stage_copy(k):
        _, _, to, _ = spot(k)
        return pltpu.make_async_copy(
            ckpt_q.at[:, :, pl.ds(pl.multiple_of(to * QCOLS, QCOLS), QCOLS)],
            stage_q.at[k], stage_q_sem.at[k],
        )

    load_k = pltpu.make_async_copy(ckpt_k, stage_kv.at[0], stage_sem.at[0])
    load_v = pltpu.make_async_copy(ckpt_v, stage_kv.at[1], stage_sem.at[1])
    load_o = pltpu.make_async_copy(ckpt_o, stage_o, stage_sem.at[2])
    load_cos = pltpu.make_async_copy(cosine, table.at[0], stage_sem.at[3])
    load_sin = pltpu.make_async_copy(sine, table.at[1], stage_sem.at[4])
    load_k.start()
    load_v.start()

    @pl.loop(0, 16)
    def _(k):
        stage_copy(k).start()

    load_o.start()
    load_cos.start()
    load_sin.start()

    barrier = pltpu.get_barrier_semaphore()

    @pl.loop(1, 16)
    def _(k):
        tx, ty, _, _ = spot(k)
        pl.semaphore_signal(barrier, inc=1, device_id=device(tx, ty, z, c), device_id_type=MESH)

    for peer in (here_up, here_down, partner, across):
        pl.semaphore_signal(barrier, inc=1, device_id=peer, device_id_type=MESH)

    load_k.wait()
    load_v.wait()
    for which in range(2):
        for g in range(8):
            mean_kv[which, g] = average(stage_kv[which, :, :, g * HEAD : (g + 1) * HEAD])

    pl.semaphore_wait(barrier, 19)

    def a2a_copy(k):
        tx, ty, _, _ = spot(k)
        return remote(
            send_w.at[k], weights.at[z, place, c], a2a_send, a2a_recv.at[k], device(tx, ty, z, c)
        )

    def piece(k):
        _, _, to, _ = spot(k)
        stage_copy(k).wait()
        return average(stage_q[k]), mean_kv[lax.rem(to, 2), lax.div(to, 2)]

    first_q, first_kv = piece(0)
    weights[z, place, c, :, :QCOLS] = first_q
    weights[z, place, c, :, QCOLS:] = first_kv

    @pl.loop(1, 16)
    def _(k):
        mean_q, mean_pair = piece(k)
        send_w[k, :, :QCOLS] = mean_q
        send_w[k, :, QCOLS:] = mean_pair

        @pl.when(k > 1)
        def _():
            a2a_copy(k - 1).start()

    sub_rows = TOK // SUB

    def hid_part(ref, at_x, j):
        return ref.at[
            pl.ds(j * sub_rows, sub_rows), pl.ds(pl.multiple_of(at_x * PIECE, PIECE), PIECE)
        ]

    def cross_copy(j):
        return remote(
            hid_part(hidden, x, j), hid_part(hid, x, j), cross_send, cross_recv.at[j], cross
        )

    def seg_copy():
        return remote(segments, seg, seg_sem.at[0], seg_sem.at[1], cross)

    local_hid = pltpu.make_async_copy(hidden, hid, hid_sem.at[0])
    local_seg = pltpu.make_async_copy(segments, seg, hid_sem.at[1])

    a2a_copy(15).start()

    @pl.when(owner)
    def _():
        @pl.loop(0, SUB)
        def _(j):
            cross_copy(j).start()

        seg_copy().start()
        local_hid.start()
        local_seg.start()

    load_o.wait()
    step = D // 8

    @pl.when(owner)
    def _():
        @pl.loop(0, 8)
        def _(j):
            cols = pl.ds(pl.multiple_of(j * step, step), step)
            weights_o[z, c, :, cols] = average(stage_o[:, :, cols])

    def swap_copy():
        return remote(
            send_o, weights_o.at[z, y_hi], swap_sem.at[0], swap_sem.at[1], across
        )

    @pl.when(jnp.logical_not(owner))
    def _():
        @pl.loop(0, 8)
        def _(j):
            cols = pl.ds(pl.multiple_of(j * step, step), step)
            send_o[:, cols] = average(stage_o[:, :, cols])

    def z_copy(level, k, direction, send_index, recv_index):
        _, _, _, source = spot(k)
        block = weights.at[level, source, c]
        return remote(
            block, block, z_send.at[send_index], z_recv.at[recv_index, k],
            here_up if direction > 0 else here_down,
        )

    def pair_copy(level, k, slot):
        _, _, _, source = spot(k)
        block = weights.at[level, source, c]
        return remote(block, block, pair_send, pair_recv.at[slot], partner)

    def pair_done(level, slot):
        block = weights.at[level, :, 1 - c]
        return remote(block, block, pair_send, pair_recv.at[slot], partner)

    def a2a_arrival(k):
        _, _, _, source = spot(k)
        block = weights.at[z, source, c]
        return remote(block, block, a2a_send, a2a_recv.at[k], partner)

    @pl.loop(0, 16)
    def _(k):
        @pl.when(k > 0)
        def _():
            a2a_arrival(k).wait_recv()

        z_copy(z, k, 1, 0, 0).start()
        z_copy(z, k, -1, 1, 1).start()
        pair_copy(z, k, 0).start()

    @pl.when(jnp.logical_not(owner))
    def _():
        swap_copy().start()

    def ring_copy(at_x, j, direction, slot):
        block = hid_part(hid, at_x, j)
        to = wrap(x + direction)
        return remote(block, block, ring_send, ring_recv.at[slot, j], device(to, y, z, c))

    east, west, far_x = wrap(x + 1), wrap(x + 3), wrap(x + 2)

    @pl.loop(0, SUB)
    def _(j):
        @pl.when(jnp.logical_not(owner))
        def _():
            cross_copy(j).wait_recv()
            ring_copy(x, j, 1, 0).start()
            ring_copy(x, j, 3, 1).start()

        @pl.loop(0, 4)
        def _(i):
            k = 4 * j + i
            z_copy(down, k, 1, 0, 0).wait_recv()

            @pl.when(lax.rem(i, 2) == 0)
            def _():
                z_copy(down, k, 1, 0, 2).start()

            pair_copy(down, k, 1).start()
            z_copy(up, k, -1, 1, 1).wait_recv()

            @pl.when(lax.rem(i, 2) == 1)
            def _():
                z_copy(up, k, -1, 1, 2).start()

            pair_copy(up, k, 2).start()

    @pl.when(jnp.logical_not(owner))
    def _():
        @pl.loop(0, SUB)
        def _(j):
            ring_copy(west, j, 1, 0).wait_recv()

            @pl.when(lax.rem(j, 2) == 0)
            def _():
                ring_copy(west, j, 1, 2).start()

            ring_copy(east, j, 3, 1).wait_recv()

            @pl.when(lax.rem(j, 2) == 1)
            def _():
                ring_copy(east, j, 3, 2).start()

    def o_block(level, core, j):
        return weights_o.at[level, core, :, pl.ds(pl.multiple_of(j * PIECE, PIECE), PIECE)]

    def zo_copy(level, j, direction, send_index, recv_index):
        block = o_block(level, c, j)
        return remote(
            block, block, zo_send.at[send_index], zo_recv.at[recv_index, j],
            here_up if direction > 0 else here_down,
        )

    def pair_o_copy(level, j, slot):
        block = o_block(level, c, j)
        return remote(block, block, pair_o_send, pair_o_recv.at[slot], partner)

    def pair_o_done(level, slot):
        block = weights_o.at[level, 1 - c]
        return remote(block, block, pair_o_send, pair_o_recv.at[slot], partner)

    @pl.when(jnp.logical_not(owner))
    def _():
        block = weights_o.at[z, c]
        remote(block, block, swap_sem.at[0], swap_sem.at[1], across).wait_recv()

    @pl.loop(0, SUB)
    def _(j):
        zo_copy(z, j, 1, 0, 0).start()
        zo_copy(z, j, -1, 1, 1).start()
        pair_o_copy(z, j, 0).start()

    @pl.loop(0, 16)
    def _(k):
        z_copy(far, k, 1, 0, 2).wait_recv()
        pair_copy(far, k, 3).start()

    @pl.when(owner)
    def _():
        local_hid.wait()
        local_seg.wait()

    @pl.when(jnp.logical_not(owner))
    def _():
        @pl.loop(0, SUB)
        def _(j):
            ring_copy(far_x, j, 1, 2).wait_recv()

        seg_copy().wait_recv()

    pair_done(z, 0).wait_recv()
    pair_done(down, 1).wait_recv()
    pair_done(up, 2).wait_recv()
    pair_done(far, 3).wait_recv()

    load_cos.wait()
    load_sin.wait()
    acc[...] = jnp.zeros_like(acc)

    def project(t, lo, hi):
        level, inner = lax.div(t, 2), lax.rem(t, 2)
        block = weights[level, pl.ds(8 * inner, 8), :, :, lo:hi].reshape(1024, hi - lo)
        rows = hid[:, pl.ds(pl.multiple_of(t * 1024, 1024), 1024)]
        acc[:, lo:hi] += jnp.dot(rows, block, preferred_element_type=jnp.float32)

    def rotate(values):
        return values * table[0] + pltpu.roll(values, HEAD // 2, 1) * table[1]

    @pl.loop(0, 8)
    def _(t):
        project(t, QCOLS, WCOLS)

    parity = lax.rem(x, 2)
    mine = acc[:, QCOLS:]
    kv[parity] = jnp.where(parity == 0, rotate(mine), mine).astype(jnp.bfloat16)

    @pl.loop(0, 8)
    def _(t):
        project(t, 0, QCOLS)

    kv_peer = device(x + 1 - 2 * parity, y, z, c)
    kv_out = remote(kv.at[parity], kv.at[parity], kv_sem.at[0], kv_sem.at[1], kv_peer)
    kv_in = remote(kv.at[1 - parity], kv.at[1 - parity], kv_sem.at[0], kv_sem.at[1], kv_peer)
    kv_out.start()
    for h in range(HEADS_CHIP):
        q_rot[h] = rotate(acc[:, h * HEAD : (h + 1) * HEAD]).astype(jnp.bfloat16)
    kv_in.wait_recv()

    segment_row = seg[...].astype(jnp.float32)
    segment_col = jnp.transpose(jnp.broadcast_to(segment_row, (HEAD, TOK)))[:, :1]
    half = TOK // 2

    def ctx_copy(place_from, h, where, slot):
        block = ctx.at[place_from, h]
        return remote(block, block, ctx_send, ctx_recv.at[slot, h], where)

    def line(h, along, by):
        on_x = lax.rem(lax.div(h, 2) + along, 2) == 0
        step_x = jnp.where(on_x, by, 0)
        step_y = jnp.where(on_x, 0, by)
        return device(wrap(x + step_x), wrap(y + step_y), z, c)

    def block_at(h, first, second):
        on_x = lax.div(h, 2) == 0
        step_x = jnp.where(on_x, first, second)
        step_y = jnp.where(on_x, second, first)
        return 4 * wrap(y + step_y) + wrap(x + step_x)

    @pl.loop(0, HEADS_CHIP)
    def _(h):
        for part in range(2):
            rows = slice(part * half, (part + 1) * half)
            width = (part + 1) * half
            scores = lax.dot_general(
                q_rot[h, rows], kv[0, :width], (((1,), (1,)), ((), ())),
                preferred_element_type=jnp.float32,
            ) * HEAD ** (-0.5)
            row_at = lax.broadcasted_iota(jnp.int32, (half, width), 0) + part * half
            col_at = lax.broadcasted_iota(jnp.int32, (half, width), 1)
            allowed = (row_at >= col_at) & (segment_col[rows] == segment_row[:, :width])
            scores = jnp.where(allowed, scores, -1e30)
            peak = jnp.max(scores, axis=-1, keepdims=True)
            raised = jnp.exp(scores - peak)
            probs = (raised * (1.0 / jnp.sum(raised, axis=-1, keepdims=True))).astype(jnp.bfloat16)
            ctx[place, h, rows] = jnp.dot(
                probs, kv[1, :width], preferred_element_type=jnp.float32
            ).astype(jnp.bfloat16)

    @pl.loop(0, HEADS_CHIP)
    def _(h):
        ctx_copy(place, h, line(h, 0, 1), 1).start()
        ctx_copy(place, h, line(h, 0, 3), 3).start()
        ctx_copy(place, h, line(h, 1, 1), 4).start()
        ctx_copy(place, h, line(h, 1, 3), 12).start()

    @pl.loop(0, SUB)
    def _(j):
        zo_copy(down, j, 1, 0, 0).wait_recv()

        @pl.when(lax.rem(j, 2) == 0)
        def _():
            zo_copy(down, j, 1, 0, 2).start()

        pair_o_copy(down, j, 1).start()
        zo_copy(up, j, -1, 1, 1).wait_recv()

        @pl.when(lax.rem(j, 2) == 1)
        def _():
            zo_copy(up, j, -1, 1, 2).start()

        pair_o_copy(up, j, 2).start()

    def ctx_wait(h, first, second, slot):
        block = ctx.at[block_at(h, first, second), h]
        remote(block, block, ctx_send, ctx_recv.at[slot, h], partner).wait_recv()

    def onward(h, slot):
        even = lax.rem(h, 2) == 0
        source = block_at(h, 3 if slot == 1 else 1, 0)

        @pl.when(even if slot == 1 else jnp.logical_not(even))
        def _():
            ctx_copy(source, h, line(h, 0, slot), 2).start()

        ctx_copy(source, h, line(h, 1, 1), 4 + slot).start()
        ctx_copy(source, h, line(h, 1, 3), 12 + slot).start()

    @pl.loop(0, HEADS_CHIP)
    def _(h):
        ctx_wait(h, 3, 0, 1)
        onward(h, 1)
        ctx_wait(h, 1, 0, 3)
        onward(h, 3)

    @pl.loop(0, HEADS_CHIP)
    def _(h):
        ctx_wait(h, 2, 0, 2)
        source = block_at(h, 2, 0)
        ctx_copy(source, h, line(h, 1, 1), 4 + 2).start()
        ctx_copy(source, h, line(h, 1, 3), 12 + 2).start()

    @pl.loop(0, 4)
    def _(i):
        t = jnp.where(i == 2, 3, jnp.where(i == 3, 2, i))
        first = wrap(N - t)

        @pl.loop(0, HEADS_CHIP)
        def _(h):
            even = lax.rem(h, 2) == 0
            ctx_wait(h, first, 3, 4 + t)

            @pl.when(even)
            def _():
                ctx_copy(block_at(h, first, 3), h, line(h, 1, 1), 8 + t).start()

            ctx_wait(h, first, 1, 12 + t)

            @pl.when(jnp.logical_not(even))
            def _():
                ctx_copy(block_at(h, first, 1), h, line(h, 1, 3), 8 + t).start()

    @pl.loop(0, SUB)
    def _(j):
        zo_copy(far, j, 1, 0, 2).wait_recv()
        pair_o_copy(far, j, 3).start()

    @pl.loop(0, 4)
    def _(t):
        @pl.loop(0, HEADS_CHIP)
        def _(h):
            ctx_wait(h, wrap(N - t), 2, 8 + t)

    pair_o_done(z, 0).wait_recv()
    pair_o_done(down, 1).wait_recv()
    pair_o_done(up, 2).wait_recv()
    pair_o_done(far, 3).wait_recv()

    acc[:, :QCOLS] = jnp.zeros((TOK, QCOLS), jnp.float32)

    @pl.loop(0, 16)
    def _(p):
        rows = jnp.concatenate([ctx[p, h] for h in range(HEADS_CHIP)], axis=1)
        cols = weights_o[:, :, :, pl.ds(pl.multiple_of(p * QCOLS, QCOLS), QCOLS)]
        acc[:, :QCOLS] += lax.dot_general(
            rows, cols.reshape(TOK, QCOLS), (((1,), (1,)), ((), ())),
            preferred_element_type=jnp.float32,
        )

    out_block[...] = acc[:, :QCOLS].astype(jnp.bfloat16)

    @pl.when(owner)
    def _():
        stay = pltpu.make_async_copy(out_block, out, out_sem.at[2])
        stay.start()
        stay.wait()

    @pl.when(jnp.logical_not(owner))
    def _():
        leave = remote(out_block, out, out_sem.at[0], out_sem.at[1], across)
        leave.start()
        leave.wait()

    def drained(ref, sem):
        remote(ref, ref, sem, kv_sem.at[1], partner).wait_send()

    drained(weights.at[0, pl.ds(0, 15), 0], a2a_send)
    for direction in range(2):
        drained(weights.at[0, pl.ds(0, 12)], z_send.at[direction])
        drained(weights_o.at[pl.ds(0, 3), 0, :, pl.ds(0, 2 * PIECE)], zo_send.at[direction])
    drained(weights.at[:, :, 0], pair_send)
    drained(weights_o.at[:, 0], pair_o_send)
    drained(kv.at[0], kv_sem.at[0])
    drained(ctx.at[pl.ds(0, 15)], ctx_send)

    @pl.when(owner)
    def _():
        drained(hid.at[:, pl.ds(0, PIECE)], cross_send)
        drained(seg, seg_sem.at[0])

    @pl.when(jnp.logical_not(owner))
    def _():
        drained(hid.at[:, pl.ds(0, 3 * PIECE)], ring_send)
        drained(send_o, swap_sem.at[0])


def tables():
    half = HEAD // 2
    freq = np.float32(rope_base) ** (
        np.float32(-2.0) * np.arange(half, dtype=np.float32) / np.float32(HEAD)
    )
    angle = np.arange(TOK, dtype=np.float32)[:, None] * freq.astype(np.float32)[None, :]
    cosine, sine = np.cos(angle), np.sin(angle)
    return (
        np.concatenate([cosine, cosine], axis=1).astype(np.float32),
        np.concatenate([-sine, sine], axis=1).astype(np.float32),
    )


def shards(ckpt_query, ckpt_key, ckpt_value, ckpt_output, hidden_in, segment_ids):
    bf16, f32 = jnp.bfloat16, jnp.float32
    dma = pltpu.SemaphoreType.DMA
    cosine, sine = tables()
    anywhere = pl.BlockSpec(memory_space=pl.ANY)
    return pl.pallas_call(
        kernel,
        out_shape=jax.ShapeDtypeStruct((TOK, TOK), bf16),
        in_specs=[anywhere] * 8,
        out_specs=anywhere,
        scratch_shapes=[
            pltpu.VMEM((16, 4, ROWS, QCOLS), bf16),
            pltpu.VMEM((2, 4, ROWS, 1024), bf16),
            pltpu.VMEM((4, ROWS, D), bf16),
            pltpu.VMEM((2, 8, ROWS, HEAD), bf16),
            pltpu.VMEM((16, ROWS, WCOLS), bf16),
            pltpu.VMEM((ROWS, D), bf16),
            pltpu.VMEM((4, 16, 2, ROWS, WCOLS), bf16),
            pltpu.VMEM((TOK, D), bf16),
            pltpu.VMEM((TOK, WCOLS), f32),
            pltpu.VMEM((4, 2, ROWS, D), bf16),
            pltpu.VMEM((16, HEADS_CHIP, TOK, HEAD), bf16),
            pltpu.VMEM((HEADS_CHIP, TOK, HEAD), bf16),
            pltpu.VMEM((2, TOK, HEAD), bf16),
            pltpu.VMEM((1, TOK), jnp.int32),
            pltpu.VMEM((2, TOK, HEAD), f32),
            pltpu.VMEM((TOK, TOK), bf16),
            dma((16,)),
            dma((5,)),
            dma,
            dma((16,)),
            dma((2,)),
            dma((3, 16)),
            dma,
            dma((4,)),
            dma((2,)),
            dma,
            dma((SUB,)),
            dma,
            dma((3, SUB)),
            dma((2,)),
            dma((2,)),
            dma((2,)),
            dma((2,)),
            dma((3, SUB)),
            dma,
            dma((4,)),
            dma,
            dma((16, HEADS_CHIP)),
            dma((3,)),
        ],
        compiler_params=pltpu.CompilerParams(
            collective_id=0, has_side_effects=True, vmem_limit_bytes=66_000_000
        ),
    )(ckpt_query, ckpt_key, ckpt_value, ckpt_output, hidden_in, segment_ids, cosine, sine)


def solution(mesh):
    placed = (
        P(None, ("dp", "head"), None),
        P(None, ("dp", "head"), None),
        P(None, ("dp", "head"), None),
        P(None, ("head", "dp"), None),
        P("dp", None),
        P("dp", None),
    )
    return jax.shard_map(
        shards, mesh=mesh, in_specs=placed, out_specs=P("dp", "head"), check_vma=False
    )
```

```python
import functools

import jax
import jax.numpy as jnp
import numpy as np
from jax import lax
from jax.experimental import pallas as pl
from jax.experimental.pallas import tpu as pltpu
from jax.sharding import PartitionSpec as P

MESH = pl.DeviceIdType.MESH
rope_base = 500000.0
N = 4
TOK = 512
HEAD = 128
HEADS_CHIP = 4
QCOLS = HEADS_CHIP * HEAD
WCOLS = QCOLS + HEAD
ROWS = 64
D = 8192
SUB = 4
PIECE = D // N
SUB_ROWS = TOK // 4
HALF = TOK // 2


def average(stack):
    return (jnp.sum(stack.astype(jnp.float32), axis=0) * 0.25).astype(jnp.bfloat16)


def wrap(value):
    return lax.rem(value, N)


def device(x, y, z, c):
    return (2 * z + lax.div(y, 2), 8 * lax.rem(y, 2) + 2 * x + c)


def kernel(
    ckpt_q, ckpt_k, ckpt_v, ckpt_o, hidden, segments, cosine, sine, out,
    stage_q, stage_kv, stage_o, mean_kv, send_w, send_o, weights, hid, acc, weights_o,
    ctx, q_rot, kv, seg, table, out_block,
    stage_q_sem, stage_sem, a2a_send, a2a_recv, z_send, z_recv, pair_send, pair_recv,
    hid_sem, cross_send, cross_recv, inner_send, inner_recv, ring_send, ring_recv, kv_sem, seg_sem,
    swap_sem, zo_send, zo_recv, pair_o_send, pair_o_recv, ctx_send, ctx_recv,
    stay_sem, leave_send, leave_recv,
):
    dp = lax.axis_index("dp")
    head = lax.axis_index("head")
    z = lax.div(dp, 2)
    y_hi = lax.rem(dp, 2)
    y = 2 * y_hi + lax.div(head, 8)
    x = wrap(lax.div(head, 2))
    c = lax.rem(head, 2)
    place = 4 * y + x
    owner = c == y_hi
    up, down, far = wrap(z + 1), wrap(z + 3), wrap(z + 2)
    here_up, here_down = device(x, y, up, c), device(x, y, down, c)
    partner = device(x, y, z, 1 - c)
    across = device(x, wrap(y + 2), z, 1 - c)
    cross = device(x, 3 - y, z, c)

    def remote(src, dst, send, recv, where):
        return pltpu.make_async_remote_copy(
            src_ref=src, dst_ref=dst, send_sem=send, recv_sem=recv,
            device_id=where, device_id_type=MESH,
        )

    def spot(k):
        dx, dy = lax.rem(k, N), lax.div(k, N)
        tx, ty = wrap(x + dx), wrap(y + dy)
        fx, fy = wrap(x + N - dx), wrap(y + N - dy)
        return tx, ty, 4 * ty + tx, 4 * fy + fx

    def stage_copy(k):
        _, _, to, _ = spot(k)
        return pltpu.make_async_copy(
            ckpt_q.at[:, :, pl.ds(pl.multiple_of(to * QCOLS, QCOLS), QCOLS)],
            stage_q.at[k], stage_q_sem.at[k],
        )

    load_k = pltpu.make_async_copy(ckpt_k, stage_kv.at[0], stage_sem.at[0])
    load_v = pltpu.make_async_copy(ckpt_v, stage_kv.at[1], stage_sem.at[1])
    load_o = pltpu.make_async_copy(ckpt_o, stage_o, stage_sem.at[2])
    load_cos = pltpu.make_async_copy(cosine, table.at[0], stage_sem.at[3])
    load_sin = pltpu.make_async_copy(sine, table.at[1], stage_sem.at[4])
    load_k.start()
    load_v.start()

    @pl.loop(0, 16)
    def _(k):
        stage_copy(k).start()

    load_o.start()
    load_cos.start()
    load_sin.start()

    barrier = pltpu.get_barrier_semaphore()

    @pl.loop(1, 16)
    def _(k):
        tx, ty, _, _ = spot(k)
        pl.semaphore_signal(barrier, inc=1, device_id=device(tx, ty, z, c), device_id_type=MESH)

    for peer in (here_up, here_down, partner, across):
        pl.semaphore_signal(barrier, inc=1, device_id=peer, device_id_type=MESH)

    load_k.wait()
    load_v.wait()
    for which in range(2):
        for g in range(8):
            mean_kv[which, g] = average(stage_kv[which, :, :, g * HEAD : (g + 1) * HEAD])

    pl.semaphore_wait(barrier, 19)

    def a2a_copy(k):
        tx, ty, _, _ = spot(k)
        return remote(
            send_w.at[k], weights.at[z, place, c], a2a_send, a2a_recv.at[k], device(tx, ty, z, c)
        )

    def piece(k):
        _, _, to, _ = spot(k)
        stage_copy(k).wait()
        return average(stage_q[k]), mean_kv[lax.rem(to, 2), lax.div(to, 2)]

    side = lax.rem(y, 2)
    inner = device(x, y + 1 - 2 * side, z, c)
    east, west, far_x = wrap(x + 1), wrap(x + 3), wrap(x + 2)

    def strip(ref, at_x, eighth, j):
        start = pl.multiple_of(at_x * PIECE + eighth * (PIECE // 2), PIECE // 2)
        return ref.at[pl.ds((j + 1) * SUB_ROWS, SUB_ROWS), pl.ds(start, PIECE // 2)]

    def top(ref, half, i):
        start = pl.multiple_of((2 * half + i) * PIECE, PIECE)
        return ref.at[pl.ds(0, SUB_ROWS), pl.ds(start, PIECE)]

    def cross_copy(j):
        return remote(
            strip(hidden, x, side, j), strip(hid, x, side, j), cross_send, cross_recv.at[j], cross
        )

    def cross_top(i):
        return remote(
            top(hidden, side, i), top(hid, side, i), cross_send, cross_recv.at[3 + i], cross
        )

    def cross_wait(j):
        block = strip(hid, x, 1 - side, j)
        remote(block, block, cross_send, cross_recv.at[j], cross).wait_recv()

    def inner_copy(j):
        block = strip(hid, x, 1 - side, j)
        return remote(block, block, inner_send, inner_recv.at[j], inner)

    def inner_wait(j):
        block = strip(hid, x, side, j)
        remote(block, block, inner_send, inner_recv.at[j], inner).wait_recv()

    def ring_copy(at_x, eighth, j, direction, slot):
        block = strip(hid, at_x, eighth, j)
        return remote(
            block, block, ring_send, ring_recv.at[slot, eighth, j],
            device(wrap(x + direction), y, z, c),
        )

    def event(number):
        if number < 3:
            cross_wait(number)
            inner_copy(number).start()
            ring_copy(x, 1 - side, number, 1, 0).start()
            ring_copy(x, 1 - side, number, 3, 1).start()
        if 1 <= number < 4:
            inner_wait(number - 1)
            ring_copy(x, side, number - 1, 1, 0).start()
            ring_copy(x, side, number - 1, 3, 1).start()
        if 3 <= number < 5:
            block = top(hid, 1 - side, number - 3)
            remote(block, block, cross_send, cross_recv.at[number], cross).wait_recv()
            remote(block, block, inner_send, inner_recv.at[number], inner).start()
        if 5 <= number < 8:
            j = number - 5

            def far_on(eighth):
                ring_copy(west, eighth, j, 1, 0).wait_recv()
                ring_copy(east, eighth, j, 3, 1).wait_recv()

            far_on(1 - side)
            far_on(side)
            ring_copy(west, 0, j, 1, 2).start()
            ring_copy(east, 1, j, 3, 2).start()

    def events(*numbers):
        @pl.when(jnp.logical_not(owner))
        def _():
            for number in numbers:
                event(number)

    def seg_copy():
        return remote(segments, seg, seg_sem.at[0], seg_sem.at[1], cross)

    local_hid = pltpu.make_async_copy(hidden, hid, hid_sem.at[0])
    local_seg = pltpu.make_async_copy(segments, seg, hid_sem.at[1])

    first_q, first_kv = piece(0)
    weights[z, place, c, :, :QCOLS] = first_q
    weights[z, place, c, :, QCOLS:] = first_kv

    @pl.loop(1, 16)
    def _(k):
        mean_q, mean_pair = piece(k)
        send_w[k, :, :QCOLS] = mean_q
        send_w[k, :, QCOLS:] = mean_pair

        @pl.when(k > 1)
        def _():
            a2a_copy(k - 1).start()

        @pl.when(owner & (lax.rem(k, 5) == 4))
        def _():
            cross_copy(lax.div(k, 5)).start()

    a2a_copy(15).start()

    @pl.when(owner)
    def _():
        cross_top(0).start()
        cross_top(1).start()
        seg_copy().start()
        local_hid.start()
        local_seg.start()

    def z_copy(level, k, direction, send_index, recv_index):
        _, _, _, source = spot(k)
        block = weights.at[level, source, c]
        return remote(
            block, block, z_send.at[send_index], z_recv.at[recv_index, k],
            here_up if direction > 0 else here_down,
        )

    def pair_copy(level, k, slot):
        _, _, _, source = spot(k)
        block = weights.at[level, source, c]
        return remote(block, block, pair_send, pair_recv.at[slot], partner)

    def pair_done(level, slot):
        block = weights.at[level, :, 1 - c]
        return remote(block, block, pair_send, pair_recv.at[slot], partner)

    def a2a_arrival(k):
        _, _, _, source = spot(k)
        block = weights.at[z, source, c]
        return remote(block, block, a2a_send, a2a_recv.at[k], partner)

    def own_part(lo, hi):
        @pl.loop(lo, hi)
        def _(k):
            @pl.when(k > 0)
            def _():
                a2a_arrival(k).wait_recv()

            z_copy(z, k, 1, 0, 0).start()
            z_copy(z, k, -1, 1, 1).start()
            pair_copy(z, k, 0).start()

    own_part(0, 8)

    load_o.wait()
    step = D // 8

    @pl.when(owner)
    def _():
        @pl.loop(0, 8)
        def _(j):
            cols = pl.ds(pl.multiple_of(j * step, step), step)
            weights_o[z, c, :, cols] = average(stage_o[:, :, cols])

    def swap_copy():
        return remote(
            send_o, weights_o.at[z, y_hi], swap_sem.at[0], swap_sem.at[1], across
        )

    @pl.when(jnp.logical_not(owner))
    def _():
        @pl.loop(0, 8)
        def _(j):
            cols = pl.ds(pl.multiple_of(j * step, step), step)
            send_o[:, cols] = average(stage_o[:, :, cols])

    events(0)
    own_part(8, 12)
    events(1)
    own_part(12, 16)
    events(2, 3)

    def pass_on(lo, hi):
        @pl.loop(lo, hi)
        def _(k):
            z_copy(down, k, 1, 0, 0).wait_recv()

            @pl.when(lax.rem(k, 2) == 0)
            def _():
                z_copy(down, k, 1, 0, 2).start()

            pair_copy(down, k, 1).start()
            z_copy(up, k, -1, 1, 1).wait_recv()

            @pl.when(lax.rem(k, 2) == 1)
            def _():
                z_copy(up, k, -1, 1, 2).start()

            pair_copy(up, k, 2).start()

    pass_on(0, 4)
    events(4)
    pass_on(4, 8)
    events(5)
    pass_on(8, 12)
    events(6)
    pass_on(12, 16)
    events(7)

    def o_block(level, core, j):
        return weights_o.at[level, core, :, pl.ds(pl.multiple_of(j * PIECE, PIECE), PIECE)]

    def zo_copy(level, j, direction, send_index, recv_index):
        block = o_block(level, c, j)
        return remote(
            block, block, zo_send.at[send_index], zo_recv.at[recv_index, j],
            here_up if direction > 0 else here_down,
        )

    def pair_o_copy(level, j, slot):
        block = o_block(level, c, j)
        return remote(block, block, pair_o_send, pair_o_recv.at[slot], partner)

    def pair_o_done(level, slot):
        block = weights_o.at[level, 1 - c]
        return remote(block, block, pair_o_send, pair_o_recv.at[slot], partner)

    @pl.when(owner)
    def _():
        local_hid.wait()
        local_seg.wait()

    @pl.when(jnp.logical_not(owner))
    def _():
        swap_copy().start()
        for i in range(2):
            block = top(hid, side, i)
            remote(block, block, inner_send, inner_recv.at[3 + i], inner).wait_recv()

        @pl.loop(0, 3)
        def _(j):
            ring_copy(far_x, 0, j, 1, 2).wait_recv()
            ring_copy(far_x, 1, j, 1, 2).wait_recv()

        seg_copy().wait_recv()

    load_cos.wait()
    load_sin.wait()
    acc[...] = jnp.zeros_like(acc)

    def project(level, lo, hi):
        block = weights[level, :, :, :, lo:hi].reshape(PIECE, hi - lo)
        rows = hid[:, pl.ds(pl.multiple_of(level * PIECE, PIECE), PIECE)]
        acc[:, lo:hi] += jnp.dot(rows, block, preferred_element_type=jnp.float32)

    def rotate(values, rows=slice(None)):
        return values * table[0, rows] + pltpu.roll(values, HEAD // 2, 1) * table[1, rows]

    parity = lax.rem(x, 2)
    kv_peer = device(x + 1 - 2 * parity, y, z, c)
    kv_out = remote(kv.at[parity], kv.at[parity], kv_sem.at[0], kv_sem.at[1], kv_peer)
    kv_in = remote(kv.at[1 - parity], kv.at[1 - parity], kv_sem.at[0], kv_sem.at[1], kv_peer)

    @pl.loop(0, 4)
    def _(i):
        level = wrap(z + jnp.where(i == 1, 3, jnp.where(i == 2, 1, jnp.where(i == 3, 2, 0))))

        @pl.loop(0, 4)
        def _(inner_k):
            k = 4 * i + inner_k
            z_copy(far, k, 1, 0, 2).wait_recv()
            pair_copy(far, k, 3).start()

        @pl.when(i == 3)
        def _():
            @pl.when(jnp.logical_not(owner))
            def _():
                block = weights_o.at[z, c]
                remote(block, block, swap_sem.at[0], swap_sem.at[1], across).wait_recv()

            @pl.loop(0, SUB)
            def _(j):
                zo_copy(z, j, 1, 0, 0).start()
                zo_copy(z, j, -1, 1, 1).start()
                pair_o_copy(z, j, 0).start()

        pair_done(level, i).wait_recv()
        project(level, QCOLS, WCOLS)

        @pl.when(i == 3)
        def _():
            mine = acc[:, QCOLS:]
            kv[parity] = jnp.where(parity == 0, rotate(mine), mine).astype(jnp.bfloat16)
            kv_out.start()

        project(level, 0, QCOLS)

    for h in range(HEADS_CHIP):
        q_rot[h] = rotate(acc[:, h * HEAD : (h + 1) * HEAD]).astype(jnp.bfloat16)
    kv_in.wait_recv()

    segment_row = seg[...].astype(jnp.float32)
    segment_col = jnp.transpose(jnp.broadcast_to(segment_row, (HEAD, TOK)))[:, :1]

    def ctx_copy(part, place_from, h, where, slot):
        block = ctx.at[part, place_from, h]
        return remote(block, block, ctx_send, ctx_recv.at[part, slot, h], where)

    def line(h, along, by):
        on_x = lax.rem(lax.div(h, 2) + along, 2) == 0
        step_x = jnp.where(on_x, by, 0)
        step_y = jnp.where(on_x, 0, by)
        return device(wrap(x + step_x), wrap(y + step_y), z, c)

    def block_at(h, first, second):
        on_x = lax.div(h, 2) == 0
        step_x = jnp.where(on_x, first, second)
        step_y = jnp.where(on_x, second, first)
        return 4 * wrap(y + step_y) + wrap(x + step_x)

    def attend(part):
        rows = slice(part * HALF, (part + 1) * HALF)
        width = (part + 1) * HALF
        row_at = lax.broadcasted_iota(jnp.int32, (HALF, width), 0) + part * HALF
        col_at = lax.broadcasted_iota(jnp.int32, (HALF, width), 1)
        allowed = (row_at >= col_at) & (segment_col[rows] == segment_row[:, :width])

        @pl.loop(0, HEADS_CHIP)
        def _(h):
            scores = lax.dot_general(
                q_rot[h, rows], kv[0, :width], (((1,), (1,)), ((), ())),
                preferred_element_type=jnp.float32,
            ) * HEAD ** (-0.5)
            scores = jnp.where(allowed, scores, -1e30)
            peak = jnp.max(scores, axis=-1, keepdims=True)
            raised = jnp.exp(scores - peak)
            probs = (raised * (1.0 / jnp.sum(raised, axis=-1, keepdims=True))).astype(jnp.bfloat16)
            ctx[part, place, h] = jnp.dot(
                probs, kv[1, :width], preferred_element_type=jnp.float32
            ).astype(jnp.bfloat16)
            ctx_copy(part, place, h, line(h, 0, 1), 1).start()
            ctx_copy(part, place, h, line(h, 0, 3), 3).start()
            ctx_copy(part, place, h, line(h, 1, 1), 4).start()
            ctx_copy(part, place, h, line(h, 1, 3), 12).start()

    def ctx_wait(part, h, first, second, slot):
        block = ctx.at[part, block_at(h, first, second), h]
        remote(block, block, ctx_send, ctx_recv.at[part, slot, h], partner).wait_recv()

    def onward(part, h, slot):
        source = block_at(h, 4 - slot, 0)

        @pl.when(lax.rem(h, 2) == (0 if slot == 1 else 1))
        def _():
            ctx_copy(part, source, h, line(h, 0, slot), 2).start()

        ctx_copy(part, source, h, line(h, 1, 1), 4 + slot).start()
        ctx_copy(part, source, h, line(h, 1, 3), 12 + slot).start()

    def first_axis(part):
        @pl.loop(0, HEADS_CHIP)
        def _(h):
            ctx_wait(part, h, 3, 0, 1)
            onward(part, h, 1)
            ctx_wait(part, h, 1, 0, 3)
            onward(part, h, 3)

    def first_axis_far(part):
        @pl.loop(0, HEADS_CHIP)
        def _(h):
            ctx_wait(part, h, 2, 0, 2)
            source = block_at(h, 2, 0)
            ctx_copy(part, source, h, line(h, 1, 1), 4 + 2).start()
            ctx_copy(part, source, h, line(h, 1, 3), 12 + 2).start()

    def second_axis(part, lo, hi):
        @pl.loop(lo, hi)
        def _(i):
            t = jnp.where(i == 2, 3, jnp.where(i == 3, 2, i))
            first = wrap(N - t)

            @pl.loop(0, HEADS_CHIP)
            def _(h):
                even = lax.rem(h, 2) == 0
                ctx_wait(part, h, first, 3, 4 + t)

                @pl.when(even)
                def _():
                    ctx_copy(part, block_at(h, first, 3), h, line(h, 1, 1), 8 + t).start()

                ctx_wait(part, h, first, 1, 12 + t)

                @pl.when(jnp.logical_not(even))
                def _():
                    ctx_copy(part, block_at(h, first, 1), h, line(h, 1, 3), 8 + t).start()

    def second_axis_far(part):
        @pl.loop(0, 4)
        def _(t):
            @pl.loop(0, HEADS_CHIP)
            def _(h):
                ctx_wait(part, h, wrap(N - t), 2, 8 + t)

    def rows_on(lo, hi):
        @pl.loop(lo, hi)
        def _(j):
            zo_copy(down, j, 1, 0, 0).wait_recv()

            @pl.when(lax.rem(j, 2) == 0)
            def _():
                zo_copy(down, j, 1, 0, 2).start()

            pair_o_copy(down, j, 1).start()
            zo_copy(up, j, -1, 1, 1).wait_recv()

            @pl.when(lax.rem(j, 2) == 1)
            def _():
                zo_copy(up, j, -1, 1, 2).start()

            pair_o_copy(up, j, 2).start()

    def combine(part, offsets):
        rows = pl.ds(part * HALF, HALF)

        @pl.loop(0, len(offsets))
        def _(i):
            offset = offsets[0]
            for at in range(1, len(offsets)):
                offset = jnp.where(i == at, offsets[at], offset)
            places = [(4 * wrap(y + offset) + along, 0) for along in range(N)]
            places += [(4 * along + wrap(x + offset), 2) for along in range(N)]
            left = jnp.concatenate(
                [ctx[part, p, first + h] for p, first in places for h in range(2)], axis=1
            )
            right = jnp.concatenate(
                [
                    weights_o[
                        :, :, :,
                        pl.ds(pl.multiple_of(p * QCOLS + first * HEAD, 2 * HEAD), 2 * HEAD),
                    ].reshape(TOK, 2 * HEAD)
                    for p, first in places
                ],
                axis=1,
            )
            acc[rows, :QCOLS] += lax.dot_general(
                left, right, (((1,), (1,)), ((), ())), preferred_element_type=jnp.float32
            )

    def deliver(part):
        rows = pl.ds(part * HALF, HALF)
        out_block[part] = acc[rows, :QCOLS].astype(jnp.bfloat16)

        @pl.when(owner)
        def _():
            pltpu.make_async_copy(out_block.at[part], out.at[rows], stay_sem.at[part]).start()

        @pl.when(jnp.logical_not(owner))
        def _():
            leave_copy(part).start()

    def leave_copy(part):
        rows = pl.ds(part * HALF, HALF)
        return remote(
            out_block.at[part], out.at[rows], leave_send.at[part], leave_recv.at[part], across
        )

    attend(0)
    attend(1)
    acc[:, :QCOLS] = jnp.zeros((TOK, QCOLS), jnp.float32)
    first_axis(0)
    rows_on(0, 2)
    first_axis_far(0)
    first_axis(1)
    second_axis(0, 0, 2)
    rows_on(2, 4)
    second_axis(0, 2, 4)
    first_axis_far(1)
    second_axis_far(0)

    @pl.loop(0, SUB)
    def _(j):
        zo_copy(far, j, 1, 0, 2).wait_recv()
        pair_o_copy(far, j, 3).start()

    second_axis(1, 0, 1)
    pair_o_done(z, 0).wait_recv()
    pair_o_done(down, 1).wait_recv()
    pair_o_done(up, 2).wait_recv()
    pair_o_done(far, 3).wait_recv()
    combine(0, (0, 1))
    second_axis(1, 1, 2)
    combine(0, (3, 2))
    deliver(0)
    second_axis(1, 2, 4)
    combine(1, (0, 1, 3))
    second_axis_far(1)
    combine(1, (2,))
    deliver(1)

    @pl.when(owner)
    def _():
        for part in range(2):
            rows = pl.ds(part * HALF, HALF)
            pltpu.make_async_copy(out_block.at[part], out.at[rows], stay_sem.at[part]).wait()

    @pl.when(jnp.logical_not(owner))
    def _():
        for part in range(2):
            leave_copy(part).wait()

    def drained(ref, sem):
        remote(ref, ref, sem, kv_sem.at[1], partner).wait_send()

    drained(weights.at[0, pl.ds(0, 15), 0], a2a_send)
    for direction in range(2):
        drained(weights.at[0, pl.ds(0, 12)], z_send.at[direction])
        drained(weights_o.at[pl.ds(0, 3), 0, :, pl.ds(0, 2 * PIECE)], zo_send.at[direction])
    drained(weights.at[:, :, 0], pair_send)
    drained(weights_o.at[:, 0], pair_o_send)
    drained(kv.at[0], kv_sem.at[0])
    drained(ctx.at[:, pl.ds(0, 15)], ctx_send)

    @pl.when(owner)
    def _():
        drained(hid.at[pl.ds(0, SUB_ROWS), pl.ds(0, 7 * PIECE // 2)], cross_send)
        drained(seg, seg_sem.at[0])

    @pl.when(jnp.logical_not(owner))
    def _():
        drained(hid.at[pl.ds(0, SUB_ROWS), pl.ds(0, 7 * PIECE // 2)], inner_send)
        drained(hid.at[pl.ds(0, 3 * SUB_ROWS), pl.ds(0, 3 * PIECE)], ring_send)
        drained(send_o, swap_sem.at[0])


def tables():
    half = HEAD // 2
    freq = np.float32(rope_base) ** (
        np.float32(-2.0) * np.arange(half, dtype=np.float32) / np.float32(HEAD)
    )
    angle = np.arange(TOK, dtype=np.float32)[:, None] * freq.astype(np.float32)[None, :]
    cosine, sine = np.cos(angle), np.sin(angle)
    return (
        np.concatenate([cosine, cosine], axis=1).astype(np.float32),
        np.concatenate([-sine, sine], axis=1).astype(np.float32),
    )


def shards(ckpt_query, ckpt_key, ckpt_value, ckpt_output, hidden_in, segment_ids):
    bf16, f32 = jnp.bfloat16, jnp.float32
    dma = pltpu.SemaphoreType.DMA
    cosine, sine = tables()
    anywhere = pl.BlockSpec(memory_space=pl.ANY)
    return pl.pallas_call(
        kernel,
        out_shape=jax.ShapeDtypeStruct((TOK, TOK), bf16),
        in_specs=[anywhere] * 8,
        out_specs=anywhere,
        scratch_shapes=[
            pltpu.VMEM((16, 4, ROWS, QCOLS), bf16),
            pltpu.VMEM((2, 4, ROWS, 1024), bf16),
            pltpu.VMEM((4, ROWS, D), bf16),
            pltpu.VMEM((2, 8, ROWS, HEAD), bf16),
            pltpu.VMEM((16, ROWS, WCOLS), bf16),
            pltpu.VMEM((ROWS, D), bf16),
            pltpu.VMEM((4, 16, 2, ROWS, WCOLS), bf16),
            pltpu.VMEM((TOK, D), bf16),
            pltpu.VMEM((TOK, WCOLS), f32),
            pltpu.VMEM((4, 2, ROWS, D), bf16),
            pltpu.VMEM((2, 16, HEADS_CHIP, HALF, HEAD), bf16),
            pltpu.VMEM((HEADS_CHIP, TOK, HEAD), bf16),
            pltpu.VMEM((2, TOK, HEAD), bf16),
            pltpu.VMEM((1, TOK), jnp.int32),
            pltpu.VMEM((2, TOK, HEAD), f32),
            pltpu.VMEM((2, HALF, TOK), bf16),
            dma((16,)),
            dma((5,)),
            dma,
            dma((16,)),
            dma((2,)),
            dma((3, 16)),
            dma,
            dma((4,)),
            dma((2,)),
            dma,
            dma((5,)),
            dma,
            dma((5,)),
            dma,
            dma((3, 2, 3)),
            dma((2,)),
            dma((2,)),
            dma((2,)),
            dma((2,)),
            dma((3, SUB)),
            dma,
            dma((4,)),
            dma,
            dma((2, 16, HEADS_CHIP)),
            dma((2,)),
            dma((2,)),
            dma((2,)),
        ],
        compiler_params=pltpu.CompilerParams(
            collective_id=0, has_side_effects=True, vmem_limit_bytes=66_000_000
        ),
    )(ckpt_query, ckpt_key, ckpt_value, ckpt_output, hidden_in, segment_ids, cosine, sine)


def solution(mesh):
    placed = (
        P(None, ("dp", "head"), None),
        P(None, ("dp", "head"), None),
        P(None, ("dp", "head"), None),
        P(None, ("head", "dp"), None),
        P("dp", None),
        P("dp", None),
    )
    return jax.shard_map(
        shards, mesh=mesh, in_specs=placed, out_specs=P("dp", "head"), check_vma=False
    )
```

```python
import functools

import jax
import jax.numpy as jnp
import numpy as np
from jax import lax
from jax.experimental import pallas as pl
from jax.experimental.pallas import tpu as pltpu
from jax.sharding import PartitionSpec as P

MESH = pl.DeviceIdType.MESH
rope_base = 500000.0
N = 4
TOK = 512
HEAD = 128
HEADS_CHIP = 4
QCOLS = HEADS_CHIP * HEAD
WCOLS = QCOLS + HEAD
ROWS = 64
D = 8192
SUB = 4
PIECE = D // N
SUB_ROWS = TOK // 4
START = (0, 384)
SIZE = (384, 128)


def average(stack):
    return (jnp.sum(stack.astype(jnp.float32), axis=0) * 0.25).astype(jnp.bfloat16)


def wrap(value):
    return lax.rem(value, N)


def device(x, y, z, c):
    return (2 * z + lax.div(y, 2), 8 * lax.rem(y, 2) + 2 * x + c)


def kernel(
    ckpt_q, ckpt_k, ckpt_v, ckpt_o, hidden, segments, cosine, sine, out,
    stage_q, stage_kv, stage_o, mean_kv, send_w, send_o, weights, hid, acc, weights_o,
    ctx, q_rot, kv, seg, table, out_block,
    stage_q_sem, stage_sem, a2a_send, a2a_recv, z_send, z_recv, pair_send, pair_recv,
    hid_sem, cross_send, cross_recv, inner_send, inner_recv, ring_send, ring_recv, kv_sem, seg_sem,
    swap_sem, zo_send, zo_recv, pair_o_send, pair_o_recv, ctx_send, ctx_recv,
    stay_sem, leave_send, leave_recv,
):
    dp = lax.axis_index("dp")
    head = lax.axis_index("head")
    z = lax.div(dp, 2)
    y_hi = lax.rem(dp, 2)
    y = 2 * y_hi + lax.div(head, 8)
    x = wrap(lax.div(head, 2))
    c = lax.rem(head, 2)
    place = 4 * y + x
    owner = c == y_hi
    up, down, far = wrap(z + 1), wrap(z + 3), wrap(z + 2)
    here_up, here_down = device(x, y, up, c), device(x, y, down, c)
    partner = device(x, y, z, 1 - c)
    across = device(x, wrap(y + 2), z, 1 - c)
    cross = device(x, 3 - y, z, c)

    def remote(src, dst, send, recv, where):
        return pltpu.make_async_remote_copy(
            src_ref=src, dst_ref=dst, send_sem=send, recv_sem=recv,
            device_id=where, device_id_type=MESH,
        )

    def spot(k):
        dx, dy = lax.rem(k, N), lax.div(k, N)
        tx, ty = wrap(x + dx), wrap(y + dy)
        fx, fy = wrap(x + N - dx), wrap(y + N - dy)
        return tx, ty, 4 * ty + tx, 4 * fy + fx

    def stage_copy(k):
        _, _, to, _ = spot(k)
        return pltpu.make_async_copy(
            ckpt_q.at[:, :, pl.ds(pl.multiple_of(to * QCOLS, QCOLS), QCOLS)],
            stage_q.at[k], stage_q_sem.at[k],
        )

    load_k = pltpu.make_async_copy(ckpt_k, stage_kv.at[0], stage_sem.at[0])
    load_v = pltpu.make_async_copy(ckpt_v, stage_kv.at[1], stage_sem.at[1])
    load_o = pltpu.make_async_copy(ckpt_o, stage_o, stage_sem.at[2])
    load_cos = pltpu.make_async_copy(cosine, table.at[0], stage_sem.at[3])
    load_sin = pltpu.make_async_copy(sine, table.at[1], stage_sem.at[4])
    load_k.start()
    load_v.start()

    @pl.loop(0, 16)
    def _(k):
        stage_copy(k).start()

    load_o.start()
    load_cos.start()
    load_sin.start()

    barrier = pltpu.get_barrier_semaphore()

    @pl.loop(1, 16)
    def _(k):
        tx, ty, _, _ = spot(k)
        pl.semaphore_signal(barrier, inc=1, device_id=device(tx, ty, z, c), device_id_type=MESH)

    for peer in (here_up, here_down, partner, across):
        pl.semaphore_signal(barrier, inc=1, device_id=peer, device_id_type=MESH)

    load_k.wait()
    load_v.wait()
    for which in range(2):
        for g in range(8):
            mean_kv[which, g] = average(stage_kv[which, :, :, g * HEAD : (g + 1) * HEAD])

    pl.semaphore_wait(barrier, 19)

    def a2a_copy(k):
        tx, ty, _, _ = spot(k)
        return remote(
            send_w.at[k], weights.at[z, place, c], a2a_send, a2a_recv.at[k], device(tx, ty, z, c)
        )

    def piece(k):
        _, _, to, _ = spot(k)
        stage_copy(k).wait()
        return average(stage_q[k]), mean_kv[lax.rem(to, 2), lax.div(to, 2)]

    side = lax.rem(y, 2)
    inner = device(x, y + 1 - 2 * side, z, c)
    east, west, far_x = wrap(x + 1), wrap(x + 3), wrap(x + 2)

    def strip(ref, at_x, eighth, j):
        start = pl.multiple_of(at_x * PIECE + eighth * (PIECE // 2), PIECE // 2)
        return ref.at[pl.ds((j + 1) * SUB_ROWS, SUB_ROWS), pl.ds(start, PIECE // 2)]

    def top(ref, half, i):
        start = pl.multiple_of((2 * half + i) * PIECE, PIECE)
        return ref.at[pl.ds(0, SUB_ROWS), pl.ds(start, PIECE)]

    def cross_copy(j):
        return remote(
            strip(hidden, x, side, j), strip(hid, x, side, j), cross_send, cross_recv.at[j], cross
        )

    def cross_top(i):
        return remote(
            top(hidden, side, i), top(hid, side, i), cross_send, cross_recv.at[3 + i], cross
        )

    def cross_wait(j):
        block = strip(hid, x, 1 - side, j)
        remote(block, block, cross_send, cross_recv.at[j], cross).wait_recv()

    def inner_copy(j):
        block = strip(hid, x, 1 - side, j)
        return remote(block, block, inner_send, inner_recv.at[j], inner)

    def inner_wait(j):
        block = strip(hid, x, side, j)
        remote(block, block, inner_send, inner_recv.at[j], inner).wait_recv()

    def ring_copy(at_x, eighth, j, direction, slot):
        block = strip(hid, at_x, eighth, j)
        return remote(
            block, block, ring_send, ring_recv.at[slot, eighth, j],
            device(wrap(x + direction), y, z, c),
        )

    def event(number):
        if number < 3:
            cross_wait(number)
            inner_copy(number).start()
            ring_copy(x, 1 - side, number, 1, 0).start()
            ring_copy(x, 1 - side, number, 3, 1).start()
        if 1 <= number < 4:
            inner_wait(number - 1)
            ring_copy(x, side, number - 1, 1, 0).start()
            ring_copy(x, side, number - 1, 3, 1).start()
        if 3 <= number < 5:
            block = top(hid, 1 - side, number - 3)
            remote(block, block, cross_send, cross_recv.at[number], cross).wait_recv()
            remote(block, block, inner_send, inner_recv.at[number], inner).start()
        if 5 <= number < 8:
            j = number - 5

            def far_on(eighth):
                ring_copy(west, eighth, j, 1, 0).wait_recv()
                ring_copy(east, eighth, j, 3, 1).wait_recv()

            far_on(1 - side)
            far_on(side)
            ring_copy(west, 0, j, 1, 2).start()
            ring_copy(east, 1, j, 3, 2).start()

    def events(*numbers):
        @pl.when(jnp.logical_not(owner))
        def _():
            for number in numbers:
                event(number)

    def seg_copy():
        return remote(segments, seg, seg_sem.at[0], seg_sem.at[1], cross)

    local_hid = pltpu.make_async_copy(hidden, hid, hid_sem.at[0])
    local_seg = pltpu.make_async_copy(segments, seg, hid_sem.at[1])

    first_q, first_kv = piece(0)
    weights[z, place, c, :, :QCOLS] = first_q
    weights[z, place, c, :, QCOLS:] = first_kv

    @pl.loop(1, 16)
    def _(k):
        mean_q, mean_pair = piece(k)
        send_w[k, :, :QCOLS] = mean_q
        send_w[k, :, QCOLS:] = mean_pair

        @pl.when(k > 1)
        def _():
            a2a_copy(k - 1).start()

        @pl.when(owner & (lax.rem(k, 5) == 4))
        def _():
            cross_copy(lax.div(k, 5)).start()

    a2a_copy(15).start()

    @pl.when(owner)
    def _():
        cross_top(0).start()
        cross_top(1).start()
        seg_copy().start()
        local_hid.start()
        local_seg.start()

    def z_copy(level, k, direction, send_index, recv_index):
        _, _, _, source = spot(k)
        block = weights.at[level, source, c]
        return remote(
            block, block, z_send.at[send_index], z_recv.at[recv_index, k],
            here_up if direction > 0 else here_down,
        )

    def pair_copy(level, k, slot):
        _, _, _, source = spot(k)
        block = weights.at[level, source, c]
        return remote(block, block, pair_send, pair_recv.at[slot], partner)

    def pair_done(level, slot):
        block = weights.at[level, :, 1 - c]
        return remote(block, block, pair_send, pair_recv.at[slot], partner)

    def a2a_arrival(k):
        _, _, _, source = spot(k)
        block = weights.at[z, source, c]
        return remote(block, block, a2a_send, a2a_recv.at[k], partner)

    def own_part(lo, hi):
        @pl.loop(lo, hi)
        def _(k):
            @pl.when(k > 0)
            def _():
                a2a_arrival(k).wait_recv()

            z_copy(z, k, 1, 0, 0).start()
            z_copy(z, k, -1, 1, 1).start()
            pair_copy(z, k, 0).start()

    own_part(0, 8)

    load_o.wait()
    step = D // 8

    @pl.when(owner)
    def _():
        @pl.loop(0, 8)
        def _(j):
            cols = pl.ds(pl.multiple_of(j * step, step), step)
            weights_o[z, c, :, cols] = average(stage_o[:, :, cols])

    def swap_copy():
        return remote(
            send_o, weights_o.at[z, y_hi], swap_sem.at[0], swap_sem.at[1], across
        )

    @pl.when(jnp.logical_not(owner))
    def _():
        @pl.loop(0, 8)
        def _(j):
            cols = pl.ds(pl.multiple_of(j * step, step), step)
            send_o[:, cols] = average(stage_o[:, :, cols])

    events(0)
    own_part(8, 12)
    events(1)
    own_part(12, 16)
    events(2, 3)

    def pass_on(lo, hi):
        @pl.loop(lo, hi)
        def _(k):
            z_copy(down, k, 1, 0, 0).wait_recv()

            @pl.when(lax.rem(k, 2) == 0)
            def _():
                z_copy(down, k, 1, 0, 2).start()

            pair_copy(down, k, 1).start()
            z_copy(up, k, -1, 1, 1).wait_recv()

            @pl.when(lax.rem(k, 2) == 1)
            def _():
                z_copy(up, k, -1, 1, 2).start()

            pair_copy(up, k, 2).start()

    pass_on(0, 4)
    events(4)
    pass_on(4, 8)
    events(5)
    pass_on(8, 12)
    events(6)
    pass_on(12, 16)
    events(7)

    def o_block(level, core, j):
        return weights_o.at[level, core, :, pl.ds(pl.multiple_of(j * PIECE, PIECE), PIECE)]

    def zo_copy(level, j, direction, send_index, recv_index):
        block = o_block(level, c, j)
        return remote(
            block, block, zo_send.at[send_index], zo_recv.at[recv_index, j],
            here_up if direction > 0 else here_down,
        )

    def pair_o_copy(level, j, slot):
        block = o_block(level, c, j)
        return remote(block, block, pair_o_send, pair_o_recv.at[slot], partner)

    def pair_o_done(level, slot):
        block = weights_o.at[level, 1 - c]
        return remote(block, block, pair_o_send, pair_o_recv.at[slot], partner)

    @pl.when(owner)
    def _():
        local_hid.wait()
        local_seg.wait()

    @pl.when(jnp.logical_not(owner))
    def _():
        swap_copy().start()
        for i in range(2):
            block = top(hid, side, i)
            remote(block, block, inner_send, inner_recv.at[3 + i], inner).wait_recv()

        @pl.loop(0, 3)
        def _(j):
            ring_copy(far_x, 0, j, 1, 2).wait_recv()
            ring_copy(far_x, 1, j, 1, 2).wait_recv()

        seg_copy().wait_recv()

    load_cos.wait()
    load_sin.wait()
    acc[...] = jnp.zeros_like(acc)

    def project(level, lo, hi):
        block = weights[level, :, :, :, lo:hi].reshape(PIECE, hi - lo)
        rows = hid[:, pl.ds(pl.multiple_of(level * PIECE, PIECE), PIECE)]
        acc[:, lo:hi] += jnp.dot(rows, block, preferred_element_type=jnp.float32)

    def rotate(values, rows=slice(None)):
        return values * table[0, rows] + pltpu.roll(values, HEAD // 2, 1) * table[1, rows]

    parity = lax.rem(x, 2)
    kv_peer = device(x + 1 - 2 * parity, y, z, c)
    kv_out = remote(kv.at[parity], kv.at[parity], kv_sem.at[0], kv_sem.at[1], kv_peer)
    kv_in = remote(kv.at[1 - parity], kv.at[1 - parity], kv_sem.at[0], kv_sem.at[1], kv_peer)

    @pl.loop(0, 4)
    def _(i):
        level = wrap(z + jnp.where(i == 1, 3, jnp.where(i == 2, 1, jnp.where(i == 3, 2, 0))))

        @pl.loop(0, 4)
        def _(inner_k):
            k = 4 * i + inner_k
            z_copy(far, k, 1, 0, 2).wait_recv()
            pair_copy(far, k, 3).start()

        @pl.when(i == 3)
        def _():
            @pl.when(jnp.logical_not(owner))
            def _():
                block = weights_o.at[z, c]
                remote(block, block, swap_sem.at[0], swap_sem.at[1], across).wait_recv()

            @pl.loop(0, SUB)
            def _(j):
                zo_copy(z, j, 1, 0, 0).start()
                zo_copy(z, j, -1, 1, 1).start()
                pair_o_copy(z, j, 0).start()

        pair_done(level, i).wait_recv()
        project(level, QCOLS, WCOLS)

        @pl.when(i == 3)
        def _():
            mine = acc[:, QCOLS:]
            kv[parity] = jnp.where(parity == 0, rotate(mine), mine).astype(jnp.bfloat16)
            kv_out.start()

        project(level, 0, QCOLS)

    for h in range(HEADS_CHIP):
        q_rot[h] = rotate(acc[:, h * HEAD : (h + 1) * HEAD]).astype(jnp.bfloat16)
    kv_in.wait_recv()

    segment_row = seg[...].astype(jnp.float32)
    segment_col = jnp.transpose(jnp.broadcast_to(segment_row, (HEAD, TOK)))[:, :1]

    def ctx_copy(part, place_from, h, where, slot):
        block = ctx.at[place_from, h, pl.ds(START[part], SIZE[part])]
        return remote(block, block, ctx_send, ctx_recv.at[part, slot, h], where)

    def line(h, along, by):
        on_x = lax.rem(lax.div(h, 2) + along, 2) == 0
        step_x = jnp.where(on_x, by, 0)
        step_y = jnp.where(on_x, 0, by)
        return device(wrap(x + step_x), wrap(y + step_y), z, c)

    def block_at(h, first, second):
        on_x = lax.div(h, 2) == 0
        step_x = jnp.where(on_x, first, second)
        step_y = jnp.where(on_x, second, first)
        return 4 * wrap(y + step_y) + wrap(x + step_x)

    def attend(part):
        width = START[part] + SIZE[part]
        rows = slice(START[part], width)
        row_at = lax.broadcasted_iota(jnp.int32, (SIZE[part], width), 0) + START[part]
        col_at = lax.broadcasted_iota(jnp.int32, (SIZE[part], width), 1)
        allowed = (row_at >= col_at) & (segment_col[rows] == segment_row[:, :width])

        @pl.loop(0, HEADS_CHIP)
        def _(h):
            scores = lax.dot_general(
                q_rot[h, rows], kv[0, :width], (((1,), (1,)), ((), ())),
                preferred_element_type=jnp.float32,
            ) * HEAD ** (-0.5)
            scores = jnp.where(allowed, scores, -1e30)
            peak = jnp.max(scores, axis=-1, keepdims=True)
            raised = jnp.exp(scores - peak)
            probs = (raised * (1.0 / jnp.sum(raised, axis=-1, keepdims=True))).astype(jnp.bfloat16)
            ctx[place, h, rows] = jnp.dot(
                probs, kv[1, :width], preferred_element_type=jnp.float32
            ).astype(jnp.bfloat16)
            ctx_copy(part, place, h, line(h, 0, 1), 1).start()
            ctx_copy(part, place, h, line(h, 0, 3), 3).start()
            ctx_copy(part, place, h, line(h, 1, 1), 4).start()
            ctx_copy(part, place, h, line(h, 1, 3), 12).start()

    def ctx_wait(part, h, first, second, slot):
        block = ctx.at[block_at(h, first, second), h, pl.ds(START[part], SIZE[part])]
        remote(block, block, ctx_send, ctx_recv.at[part, slot, h], partner).wait_recv()

    def onward(part, h, slot):
        source = block_at(h, 4 - slot, 0)

        @pl.when(lax.rem(h, 2) == (0 if slot == 1 else 1))
        def _():
            ctx_copy(part, source, h, line(h, 0, slot), 2).start()

        ctx_copy(part, source, h, line(h, 1, 1), 4 + slot).start()
        ctx_copy(part, source, h, line(h, 1, 3), 12 + slot).start()

    def first_axis(part):
        @pl.loop(0, HEADS_CHIP)
        def _(h):
            ctx_wait(part, h, 3, 0, 1)
            onward(part, h, 1)
            ctx_wait(part, h, 1, 0, 3)
            onward(part, h, 3)

    def first_axis_far(part):
        @pl.loop(0, HEADS_CHIP)
        def _(h):
            ctx_wait(part, h, 2, 0, 2)
            source = block_at(h, 2, 0)
            ctx_copy(part, source, h, line(h, 1, 1), 4 + 2).start()
            ctx_copy(part, source, h, line(h, 1, 3), 12 + 2).start()

    def second_axis(part, lo, hi):
        @pl.loop(lo, hi)
        def _(i):
            t = jnp.where(i == 2, 3, jnp.where(i == 3, 2, i))
            first = wrap(N - t)

            @pl.loop(0, HEADS_CHIP)
            def _(h):
                even = lax.rem(h, 2) == 0
                ctx_wait(part, h, first, 3, 4 + t)

                @pl.when(even)
                def _():
                    ctx_copy(part, block_at(h, first, 3), h, line(h, 1, 1), 8 + t).start()

                ctx_wait(part, h, first, 1, 12 + t)

                @pl.when(jnp.logical_not(even))
                def _():
                    ctx_copy(part, block_at(h, first, 1), h, line(h, 1, 3), 8 + t).start()

    def second_axis_far(part):
        @pl.loop(0, 4)
        def _(t):
            @pl.loop(0, HEADS_CHIP)
            def _(h):
                ctx_wait(part, h, wrap(N - t), 2, 8 + t)

    def rows_on(lo, hi):
        @pl.loop(lo, hi)
        def _(j):
            zo_copy(down, j, 1, 0, 0).wait_recv()

            @pl.when(lax.rem(j, 2) == 0)
            def _():
                zo_copy(down, j, 1, 0, 2).start()

            pair_o_copy(down, j, 1).start()
            zo_copy(up, j, -1, 1, 1).wait_recv()

            @pl.when(lax.rem(j, 2) == 1)
            def _():
                zo_copy(up, j, -1, 1, 2).start()

            pair_o_copy(up, j, 2).start()

    def combine(part, offsets):
        rows = pl.ds(START[part], SIZE[part])

        @pl.loop(0, len(offsets))
        def _(i):
            offset = offsets[0]
            for at in range(1, len(offsets)):
                offset = jnp.where(i == at, offsets[at], offset)
            places = [(4 * wrap(y + offset) + along, 0) for along in range(N)]
            places += [(4 * along + wrap(x + offset), 2) for along in range(N)]
            left = jnp.concatenate(
                [ctx[p, first + h, rows] for p, first in places for h in range(2)], axis=1
            )
            right = jnp.concatenate(
                [
                    weights_o[
                        :, :, :,
                        pl.ds(pl.multiple_of(p * QCOLS + first * HEAD, 2 * HEAD), 2 * HEAD),
                    ].reshape(TOK, 2 * HEAD)
                    for p, first in places
                ],
                axis=1,
            )
            acc[rows, :QCOLS] += lax.dot_general(
                left, right, (((1,), (1,)), ((), ())), preferred_element_type=jnp.float32
            )

    def deliver(part):
        rows = pl.ds(START[part], SIZE[part])
        out_block[rows] = acc[rows, :QCOLS].astype(jnp.bfloat16)

        @pl.when(owner)
        def _():
            pltpu.make_async_copy(out_block.at[rows], out.at[rows], stay_sem.at[part]).start()

        @pl.when(jnp.logical_not(owner))
        def _():
            leave_copy(part).start()

    def leave_copy(part):
        rows = pl.ds(START[part], SIZE[part])
        return remote(
            out_block.at[rows], out.at[rows], leave_send.at[part], leave_recv.at[part], across
        )

    attend(0)
    attend(1)
    acc[:, :QCOLS] = jnp.zeros((TOK, QCOLS), jnp.float32)
    first_axis(0)
    rows_on(0, 2)
    first_axis_far(0)
    first_axis(1)
    second_axis(0, 0, 2)
    rows_on(2, 4)
    second_axis(0, 2, 4)
    first_axis_far(1)
    second_axis_far(0)

    @pl.loop(0, SUB)
    def _(j):
        zo_copy(far, j, 1, 0, 2).wait_recv()
        pair_o_copy(far, j, 3).start()

    second_axis(1, 0, 1)
    pair_o_done(z, 0).wait_recv()
    pair_o_done(down, 1).wait_recv()
    pair_o_done(up, 2).wait_recv()
    pair_o_done(far, 3).wait_recv()
    combine(0, (0, 1))
    second_axis(1, 1, 2)
    combine(0, (3, 2))
    deliver(0)
    second_axis(1, 2, 4)
    combine(1, (0, 1, 3))
    second_axis_far(1)
    combine(1, (2,))
    deliver(1)

    @pl.when(owner)
    def _():
        for part in range(2):
            rows = pl.ds(START[part], SIZE[part])
            pltpu.make_async_copy(out_block.at[rows], out.at[rows], stay_sem.at[part]).wait()

    @pl.when(jnp.logical_not(owner))
    def _():
        for part in range(2):
            leave_copy(part).wait()

    def drained(ref, sem):
        remote(ref, ref, sem, kv_sem.at[1], partner).wait_send()

    drained(weights.at[0, pl.ds(0, 15), 0], a2a_send)
    for direction in range(2):
        drained(weights.at[0, pl.ds(0, 12)], z_send.at[direction])
        drained(weights_o.at[pl.ds(0, 3), 0, :, pl.ds(0, 2 * PIECE)], zo_send.at[direction])
    drained(weights.at[:, :, 0], pair_send)
    drained(weights_o.at[:, 0], pair_o_send)
    drained(kv.at[0], kv_sem.at[0])
    drained(ctx.at[pl.ds(0, 15)], ctx_send)

    @pl.when(owner)
    def _():
        drained(hid.at[pl.ds(0, SUB_ROWS), pl.ds(0, 7 * PIECE // 2)], cross_send)
        drained(seg, seg_sem.at[0])

    @pl.when(jnp.logical_not(owner))
    def _():
        drained(hid.at[pl.ds(0, SUB_ROWS), pl.ds(0, 7 * PIECE // 2)], inner_send)
        drained(hid.at[pl.ds(0, 3 * SUB_ROWS), pl.ds(0, 3 * PIECE)], ring_send)
        drained(send_o, swap_sem.at[0])


def tables():
    half = HEAD // 2
    freq = np.float32(rope_base) ** (
        np.float32(-2.0) * np.arange(half, dtype=np.float32) / np.float32(HEAD)
    )
    angle = np.arange(TOK, dtype=np.float32)[:, None] * freq.astype(np.float32)[None, :]
    cosine, sine = np.cos(angle), np.sin(angle)
    return (
        np.concatenate([cosine, cosine], axis=1).astype(np.float32),
        np.concatenate([-sine, sine], axis=1).astype(np.float32),
    )


def shards(ckpt_query, ckpt_key, ckpt_value, ckpt_output, hidden_in, segment_ids):
    bf16, f32 = jnp.bfloat16, jnp.float32
    dma = pltpu.SemaphoreType.DMA
    cosine, sine = tables()
    anywhere = pl.BlockSpec(memory_space=pl.ANY)
    return pl.pallas_call(
        kernel,
        out_shape=jax.ShapeDtypeStruct((TOK, TOK), bf16),
        in_specs=[anywhere] * 8,
        out_specs=anywhere,
        scratch_shapes=[
            pltpu.VMEM((16, 4, ROWS, QCOLS), bf16),
            pltpu.VMEM((2, 4, ROWS, 1024), bf16),
            pltpu.VMEM((4, ROWS, D), bf16),
            pltpu.VMEM((2, 8, ROWS, HEAD), bf16),
            pltpu.VMEM((16, ROWS, WCOLS), bf16),
            pltpu.VMEM((ROWS, D), bf16),
            pltpu.VMEM((4, 16, 2, ROWS, WCOLS), bf16),
            pltpu.VMEM((TOK, D), bf16),
            pltpu.VMEM((TOK, WCOLS), f32),
            pltpu.VMEM((4, 2, ROWS, D), bf16),
            pltpu.VMEM((16, HEADS_CHIP, TOK, HEAD), bf16),
            pltpu.VMEM((HEADS_CHIP, TOK, HEAD), bf16),
            pltpu.VMEM((2, TOK, HEAD), bf16),
            pltpu.VMEM((1, TOK), jnp.int32),
            pltpu.VMEM((2, TOK, HEAD), f32),
            pltpu.VMEM((TOK, TOK), bf16),
            dma((16,)),
            dma((5,)),
            dma,
            dma((16,)),
            dma((2,)),
            dma((3, 16)),
            dma,
            dma((4,)),
            dma((2,)),
            dma,
            dma((5,)),
            dma,
            dma((5,)),
            dma,
            dma((3, 2, 3)),
            dma((2,)),
            dma((2,)),
            dma((2,)),
            dma((2,)),
            dma((3, SUB)),
            dma,
            dma((4,)),
            dma,
            dma((2, 16, HEADS_CHIP)),
            dma((2,)),
            dma((2,)),
            dma((2,)),
        ],
        compiler_params=pltpu.CompilerParams(
            collective_id=0, has_side_effects=True, vmem_limit_bytes=66_000_000
        ),
    )(ckpt_query, ckpt_key, ckpt_value, ckpt_output, hidden_in, segment_ids, cosine, sine)


def solution(mesh):
    placed = (
        P(None, ("dp", "head"), None),
        P(None, ("dp", "head"), None),
        P(None, ("dp", "head"), None),
        P(None, ("head", "dp"), None),
        P("dp", None),
        P("dp", None),
    )
    return jax.shard_map(
        shards, mesh=mesh, in_specs=placed, out_specs=P("dp", "head"), check_vma=False
    )
```

```python
import functools

import jax
import jax.numpy as jnp
import numpy as np
from jax import lax
from jax.experimental import pallas as pl
from jax.experimental.pallas import tpu as pltpu
from jax.sharding import PartitionSpec as P

MESH = pl.DeviceIdType.MESH
rope_base = 500000.0
N = 4
TOK = 512
HEAD = 128
HEADS_CHIP = 4
QCOLS = HEADS_CHIP * HEAD
WCOLS = QCOLS + HEAD
ROWS = 64
D = 8192
SUB = 4
PIECE = D // N
SUB_ROWS = TOK // 4
START = (0, 192)
SIZE = (192, 320)


def average(stack):
    return (jnp.sum(stack.astype(jnp.float32), axis=0) * 0.25).astype(jnp.bfloat16)


def wrap(value):
    return lax.rem(value, N)


def device(x, y, z, c):
    return (2 * z + lax.div(y, 2), 8 * lax.rem(y, 2) + 2 * x + c)


def kernel(
    ckpt_q, ckpt_k, ckpt_v, ckpt_o, hidden, segments, cosine, sine, out,
    stage_q, stage_kv, stage_o, mean_kv, send_w, send_o, weights, hid, acc, weights_o,
    ctx, q_rot, kv, seg, table, out_block,
    stage_q_sem, stage_sem, a2a_send, a2a_recv, z_send, z_recv, pair_send, pair_recv,
    hid_sem, cross_send, cross_recv, inner_send, inner_recv, ring_send, ring_recv, kv_sem, seg_sem,
    swap_sem, zo_send, zo_recv, pair_o_send, pair_o_recv, ctx_send, ctx_recv,
    stay_sem, leave_send, leave_recv,
):
    dp = lax.axis_index("dp")
    head = lax.axis_index("head")
    z = lax.div(dp, 2)
    y_hi = lax.rem(dp, 2)
    y = 2 * y_hi + lax.div(head, 8)
    x = wrap(lax.div(head, 2))
    c = lax.rem(head, 2)
    place = 4 * y + x
    owner = c == y_hi
    up, down, far = wrap(z + 1), wrap(z + 3), wrap(z + 2)
    here_up, here_down = device(x, y, up, c), device(x, y, down, c)
    partner = device(x, y, z, 1 - c)
    across = device(x, wrap(y + 2), z, 1 - c)
    cross = device(x, 3 - y, z, c)

    def remote(src, dst, send, recv, where):
        return pltpu.make_async_remote_copy(
            src_ref=src, dst_ref=dst, send_sem=send, recv_sem=recv,
            device_id=where, device_id_type=MESH,
        )

    def spot(k):
        dx, dy = lax.rem(k, N), lax.div(k, N)
        tx, ty = wrap(x + dx), wrap(y + dy)
        fx, fy = wrap(x + N - dx), wrap(y + N - dy)
        return tx, ty, 4 * ty + tx, 4 * fy + fx

    def stage_copy(k):
        _, _, to, _ = spot(k)
        return pltpu.make_async_copy(
            ckpt_q.at[:, :, pl.ds(pl.multiple_of(to * QCOLS, QCOLS), QCOLS)],
            stage_q.at[k], stage_q_sem.at[k],
        )

    load_k = pltpu.make_async_copy(ckpt_k, stage_kv.at[0], stage_sem.at[0])
    load_v = pltpu.make_async_copy(ckpt_v, stage_kv.at[1], stage_sem.at[1])
    load_o = pltpu.make_async_copy(ckpt_o, stage_o, stage_sem.at[2])
    load_cos = pltpu.make_async_copy(cosine, table.at[0], stage_sem.at[3])
    load_sin = pltpu.make_async_copy(sine, table.at[1], stage_sem.at[4])
    load_k.start()
    load_v.start()

    @pl.loop(0, 16)
    def _(k):
        stage_copy(k).start()

    load_o.start()
    load_cos.start()
    load_sin.start()

    barrier = pltpu.get_barrier_semaphore()

    @pl.loop(1, 16)
    def _(k):
        tx, ty, _, _ = spot(k)
        pl.semaphore_signal(barrier, inc=1, device_id=device(tx, ty, z, c), device_id_type=MESH)

    for peer in (here_up, here_down, partner, across):
        pl.semaphore_signal(barrier, inc=1, device_id=peer, device_id_type=MESH)

    load_k.wait()
    load_v.wait()
    for which in range(2):
        for g in range(8):
            mean_kv[which, g] = average(stage_kv[which, :, :, g * HEAD : (g + 1) * HEAD])

    pl.semaphore_wait(barrier, 19)

    def a2a_copy(k):
        tx, ty, _, _ = spot(k)
        return remote(
            send_w.at[k], weights.at[z, place, c], a2a_send, a2a_recv.at[k], device(tx, ty, z, c)
        )

    def piece(k):
        _, _, to, _ = spot(k)
        stage_copy(k).wait()
        return average(stage_q[k]), mean_kv[lax.rem(to, 2), lax.div(to, 2)]

    side = lax.rem(y, 2)
    inner = device(x, y + 1 - 2 * side, z, c)
    east, west, far_x = wrap(x + 1), wrap(x + 3), wrap(x + 2)

    def strip(ref, at_x, eighth, j):
        start = pl.multiple_of(at_x * PIECE + eighth * (PIECE // 2), PIECE // 2)
        return ref.at[pl.ds((j + 1) * SUB_ROWS, SUB_ROWS), pl.ds(start, PIECE // 2)]

    def top(ref, half, i):
        start = pl.multiple_of((2 * half + i) * PIECE, PIECE)
        return ref.at[pl.ds(0, SUB_ROWS), pl.ds(start, PIECE)]

    def cross_copy(j):
        return remote(
            strip(hidden, x, side, j), strip(hid, x, side, j), cross_send, cross_recv.at[j], cross
        )

    def cross_top(i):
        return remote(
            top(hidden, side, i), top(hid, side, i), cross_send, cross_recv.at[3 + i], cross
        )

    def cross_wait(j):
        block = strip(hid, x, 1 - side, j)
        remote(block, block, cross_send, cross_recv.at[j], cross).wait_recv()

    def inner_copy(j):
        block = strip(hid, x, 1 - side, j)
        return remote(block, block, inner_send, inner_recv.at[j], inner)

    def inner_wait(j):
        block = strip(hid, x, side, j)
        remote(block, block, inner_send, inner_recv.at[j], inner).wait_recv()

    def ring_copy(at_x, eighth, j, direction, slot):
        block = strip(hid, at_x, eighth, j)
        return remote(
            block, block, ring_send, ring_recv.at[slot, eighth, j],
            device(wrap(x + direction), y, z, c),
        )

    def event(number):
        if number < 3:
            cross_wait(number)
            inner_copy(number).start()
            ring_copy(x, 1 - side, number, 1, 0).start()
            ring_copy(x, 1 - side, number, 3, 1).start()
        if 1 <= number < 4:
            inner_wait(number - 1)
            ring_copy(x, side, number - 1, 1, 0).start()
            ring_copy(x, side, number - 1, 3, 1).start()
        if 3 <= number < 5:
            block = top(hid, 1 - side, number - 3)
            remote(block, block, cross_send, cross_recv.at[number], cross).wait_recv()
            remote(block, block, inner_send, inner_recv.at[number], inner).start()
        if 5 <= number < 8:
            j = number - 5

            def far_on(eighth):
                ring_copy(west, eighth, j, 1, 0).wait_recv()
                ring_copy(east, eighth, j, 3, 1).wait_recv()

            far_on(1 - side)
            far_on(side)
            ring_copy(west, 0, j, 1, 2).start()
            ring_copy(east, 1, j, 3, 2).start()

    def events(*numbers):
        @pl.when(jnp.logical_not(owner))
        def _():
            for number in numbers:
                event(number)

    def seg_copy():
        return remote(segments, seg, seg_sem.at[0], seg_sem.at[1], cross)

    local_hid = pltpu.make_async_copy(hidden, hid, hid_sem.at[0])
    local_seg = pltpu.make_async_copy(segments, seg, hid_sem.at[1])

    first_q, first_kv = piece(0)
    weights[z, place, c, :, :QCOLS] = first_q
    weights[z, place, c, :, QCOLS:] = first_kv

    @pl.loop(1, 16)
    def _(k):
        mean_q, mean_pair = piece(k)
        send_w[k, :, :QCOLS] = mean_q
        send_w[k, :, QCOLS:] = mean_pair

        @pl.when(k > 1)
        def _():
            a2a_copy(k - 1).start()

        @pl.when(owner & (lax.rem(k, 5) == 4))
        def _():
            cross_copy(lax.div(k, 5)).start()

    a2a_copy(15).start()

    @pl.when(owner)
    def _():
        cross_top(0).start()
        cross_top(1).start()
        seg_copy().start()
        local_hid.start()
        local_seg.start()

    def z_copy(level, k, direction, send_index, recv_index):
        _, _, _, source = spot(k)
        block = weights.at[level, source, c]
        return remote(
            block, block, z_send.at[send_index], z_recv.at[recv_index, k],
            here_up if direction > 0 else here_down,
        )

    def pair_copy(level, k, slot):
        _, _, _, source = spot(k)
        block = weights.at[level, source, c]
        return remote(block, block, pair_send, pair_recv.at[slot], partner)

    def pair_done(level, slot):
        block = weights.at[level, :, 1 - c]
        return remote(block, block, pair_send, pair_recv.at[slot], partner)

    def a2a_arrival(k):
        _, _, _, source = spot(k)
        block = weights.at[z, source, c]
        return remote(block, block, a2a_send, a2a_recv.at[k], partner)

    def own_part(lo, hi):
        @pl.loop(lo, hi)
        def _(k):
            @pl.when(k > 0)
            def _():
                a2a_arrival(k).wait_recv()

            z_copy(z, k, 1, 0, 0).start()
            z_copy(z, k, -1, 1, 1).start()
            pair_copy(z, k, 0).start()

    own_part(0, 8)

    load_o.wait()
    step = D // 8

    @pl.when(owner)
    def _():
        @pl.loop(0, 8)
        def _(j):
            cols = pl.ds(pl.multiple_of(j * step, step), step)
            weights_o[z, c, :, cols] = average(stage_o[:, :, cols])

    def swap_copy():
        return remote(
            send_o, weights_o.at[z, y_hi], swap_sem.at[0], swap_sem.at[1], across
        )

    @pl.when(jnp.logical_not(owner))
    def _():
        @pl.loop(0, 8)
        def _(j):
            cols = pl.ds(pl.multiple_of(j * step, step), step)
            send_o[:, cols] = average(stage_o[:, :, cols])

    events(0)
    own_part(8, 12)
    events(1)
    own_part(12, 16)
    events(2, 3)

    def pass_on(lo, hi):
        @pl.loop(lo, hi)
        def _(k):
            z_copy(down, k, 1, 0, 0).wait_recv()

            @pl.when(lax.rem(k, 2) == 0)
            def _():
                z_copy(down, k, 1, 0, 2).start()

            pair_copy(down, k, 1).start()
            z_copy(up, k, -1, 1, 1).wait_recv()

            @pl.when(lax.rem(k, 2) == 1)
            def _():
                z_copy(up, k, -1, 1, 2).start()

            pair_copy(up, k, 2).start()

    pass_on(0, 4)
    events(4)
    pass_on(4, 8)
    events(5)
    pass_on(8, 12)
    events(6)
    pass_on(12, 16)
    events(7)

    def o_block(level, core, j):
        return weights_o.at[level, core, :, pl.ds(pl.multiple_of(j * PIECE, PIECE), PIECE)]

    def zo_copy(level, j, direction, send_index, recv_index):
        block = o_block(level, c, j)
        return remote(
            block, block, zo_send.at[send_index], zo_recv.at[recv_index, j],
            here_up if direction > 0 else here_down,
        )

    def pair_o_copy(level, j, slot):
        block = o_block(level, c, j)
        return remote(block, block, pair_o_send, pair_o_recv.at[slot], partner)

    def pair_o_done(level, slot):
        block = weights_o.at[level, 1 - c]
        return remote(block, block, pair_o_send, pair_o_recv.at[slot], partner)

    @pl.when(owner)
    def _():
        local_hid.wait()
        local_seg.wait()

    @pl.when(jnp.logical_not(owner))
    def _():
        swap_copy().start()
        for i in range(2):
            block = top(hid, side, i)
            remote(block, block, inner_send, inner_recv.at[3 + i], inner).wait_recv()

        @pl.loop(0, 3)
        def _(j):
            ring_copy(far_x, 0, j, 1, 2).wait_recv()
            ring_copy(far_x, 1, j, 1, 2).wait_recv()

        seg_copy().wait_recv()

    load_cos.wait()
    load_sin.wait()
    acc[...] = jnp.zeros_like(acc)

    def project(level, lo, hi):
        block = weights[level, :, :, :, lo:hi].reshape(PIECE, hi - lo)
        rows = hid[:, pl.ds(pl.multiple_of(level * PIECE, PIECE), PIECE)]
        acc[:, lo:hi] += jnp.dot(rows, block, preferred_element_type=jnp.float32)

    def rotate(values, rows=slice(None)):
        return values * table[0, rows] + pltpu.roll(values, HEAD // 2, 1) * table[1, rows]

    parity = lax.rem(x, 2)
    kv_peer = device(x + 1 - 2 * parity, y, z, c)
    kv_out = remote(kv.at[parity], kv.at[parity], kv_sem.at[0], kv_sem.at[1], kv_peer)
    kv_in = remote(kv.at[1 - parity], kv.at[1 - parity], kv_sem.at[0], kv_sem.at[1], kv_peer)

    @pl.loop(0, 4)
    def _(i):
        level = wrap(z + jnp.where(i == 1, 3, jnp.where(i == 2, 1, jnp.where(i == 3, 2, 0))))

        @pl.loop(0, 4)
        def _(inner_k):
            k = 4 * i + inner_k
            z_copy(far, k, 1, 0, 2).wait_recv()
            pair_copy(far, k, 3).start()

        @pl.when(i == 3)
        def _():
            @pl.when(jnp.logical_not(owner))
            def _():
                block = weights_o.at[z, c]
                remote(block, block, swap_sem.at[0], swap_sem.at[1], across).wait_recv()

            @pl.loop(0, SUB)
            def _(j):
                zo_copy(z, j, 1, 0, 0).start()
                zo_copy(z, j, -1, 1, 1).start()
                pair_o_copy(z, j, 0).start()

        pair_done(level, i).wait_recv()
        project(level, QCOLS, WCOLS)

        @pl.when(i == 3)
        def _():
            mine = acc[:, QCOLS:]
            kv[parity] = jnp.where(parity == 0, rotate(mine), mine).astype(jnp.bfloat16)
            kv_out.start()

        project(level, 0, QCOLS)

    for h in range(HEADS_CHIP):
        q_rot[h] = rotate(acc[:, h * HEAD : (h + 1) * HEAD]).astype(jnp.bfloat16)
    kv_in.wait_recv()

    segment_row = seg[...].astype(jnp.float32)
    segment_col = jnp.transpose(jnp.broadcast_to(segment_row, (HEAD, TOK)))[:, :1]

    def ctx_copy(part, place_from, h, where, slot):
        block = ctx.at[place_from, h, pl.ds(START[part], SIZE[part])]
        return remote(block, block, ctx_send, ctx_recv.at[part, slot, h], where)

    def line(h, along, by):
        on_x = lax.rem(lax.div(h, 2) + along, 2) == 0
        step_x = jnp.where(on_x, by, 0)
        step_y = jnp.where(on_x, 0, by)
        return device(wrap(x + step_x), wrap(y + step_y), z, c)

    def block_at(h, first, second):
        on_x = lax.div(h, 2) == 0
        step_x = jnp.where(on_x, first, second)
        step_y = jnp.where(on_x, second, first)
        return 4 * wrap(y + step_y) + wrap(x + step_x)

    def attend(part):
        width = START[part] + SIZE[part]
        rows = slice(START[part], width)
        row_at = lax.broadcasted_iota(jnp.int32, (SIZE[part], width), 0) + START[part]
        col_at = lax.broadcasted_iota(jnp.int32, (SIZE[part], width), 1)
        allowed = (row_at >= col_at) & (segment_col[rows] == segment_row[:, :width])

        @pl.loop(0, HEADS_CHIP)
        def _(h):
            scores = lax.dot_general(
                q_rot[h, rows], kv[0, :width], (((1,), (1,)), ((), ())),
                preferred_element_type=jnp.float32,
            ) * HEAD ** (-0.5)
            scores = jnp.where(allowed, scores, -1e30)
            peak = jnp.max(scores, axis=-1, keepdims=True)
            raised = jnp.exp(scores - peak)
            probs = (raised * (1.0 / jnp.sum(raised, axis=-1, keepdims=True))).astype(jnp.bfloat16)
            ctx[place, h, rows] = jnp.dot(
                probs, kv[1, :width], preferred_element_type=jnp.float32
            ).astype(jnp.bfloat16)
            ctx_copy(part, place, h, line(h, 0, 1), 1).start()
            ctx_copy(part, place, h, line(h, 0, 3), 3).start()
            ctx_copy(part, place, h, line(h, 1, 1), 4).start()
            ctx_copy(part, place, h, line(h, 1, 3), 12).start()

    def ctx_wait(part, h, first, second, slot):
        block = ctx.at[block_at(h, first, second), h, pl.ds(START[part], SIZE[part])]
        remote(block, block, ctx_send, ctx_recv.at[part, slot, h], partner).wait_recv()

    def onward(part, h, slot):
        source = block_at(h, 4 - slot, 0)

        @pl.when(lax.rem(h, 2) == (0 if slot == 1 else 1))
        def _():
            ctx_copy(part, source, h, line(h, 0, slot), 2).start()

        ctx_copy(part, source, h, line(h, 1, 1), 4 + slot).start()
        ctx_copy(part, source, h, line(h, 1, 3), 12 + slot).start()

    def first_axis(part):
        @pl.loop(0, HEADS_CHIP)
        def _(h):
            ctx_wait(part, h, 3, 0, 1)
            onward(part, h, 1)
            ctx_wait(part, h, 1, 0, 3)
            onward(part, h, 3)

    def first_axis_far(part):
        @pl.loop(0, HEADS_CHIP)
        def _(h):
            ctx_wait(part, h, 2, 0, 2)
            source = block_at(h, 2, 0)
            ctx_copy(part, source, h, line(h, 1, 1), 4 + 2).start()
            ctx_copy(part, source, h, line(h, 1, 3), 12 + 2).start()

    def second_axis(part, lo, hi):
        @pl.loop(lo, hi)
        def _(i):
            t = jnp.where(i == 2, 3, jnp.where(i == 3, 2, i))
            first = wrap(N - t)

            @pl.loop(0, HEADS_CHIP)
            def _(h):
                even = lax.rem(h, 2) == 0
                ctx_wait(part, h, first, 3, 4 + t)

                @pl.when(even)
                def _():
                    ctx_copy(part, block_at(h, first, 3), h, line(h, 1, 1), 8 + t).start()

                ctx_wait(part, h, first, 1, 12 + t)

                @pl.when(jnp.logical_not(even))
                def _():
                    ctx_copy(part, block_at(h, first, 1), h, line(h, 1, 3), 8 + t).start()

    def second_axis_far(part):
        @pl.loop(0, 4)
        def _(t):
            @pl.loop(0, HEADS_CHIP)
            def _(h):
                ctx_wait(part, h, wrap(N - t), 2, 8 + t)

    def rows_on(lo, hi):
        @pl.loop(lo, hi)
        def _(j):
            zo_copy(down, j, 1, 0, 0).wait_recv()

            @pl.when(lax.rem(j, 2) == 0)
            def _():
                zo_copy(down, j, 1, 0, 2).start()

            pair_o_copy(down, j, 1).start()
            zo_copy(up, j, -1, 1, 1).wait_recv()

            @pl.when(lax.rem(j, 2) == 1)
            def _():
                zo_copy(up, j, -1, 1, 2).start()

            pair_o_copy(up, j, 2).start()

    def combine(part, offsets):
        rows = pl.ds(START[part], SIZE[part])

        @pl.loop(0, len(offsets))
        def _(i):
            offset = offsets[0]
            for at in range(1, len(offsets)):
                offset = jnp.where(i == at, offsets[at], offset)
            places = [(4 * wrap(y + offset) + along, 0) for along in range(N)]
            places += [(4 * along + wrap(x + offset), 2) for along in range(N)]
            left = jnp.concatenate(
                [ctx[p, first + h, rows] for p, first in places for h in range(2)], axis=1
            )
            right = jnp.concatenate(
                [
                    weights_o[
                        :, :, :,
                        pl.ds(pl.multiple_of(p * QCOLS + first * HEAD, 2 * HEAD), 2 * HEAD),
                    ].reshape(TOK, 2 * HEAD)
                    for p, first in places
                ],
                axis=1,
            )
            acc[rows, :QCOLS] += lax.dot_general(
                left, right, (((1,), (1,)), ((), ())), preferred_element_type=jnp.float32
            )

    def deliver(part):
        rows = pl.ds(START[part], SIZE[part])
        out_block[rows] = acc[rows, :QCOLS].astype(jnp.bfloat16)

        @pl.when(owner)
        def _():
            pltpu.make_async_copy(out_block.at[rows], out.at[rows], stay_sem.at[part]).start()

        @pl.when(jnp.logical_not(owner))
        def _():
            leave_copy(part).start()

    def leave_copy(part):
        rows = pl.ds(START[part], SIZE[part])
        return remote(
            out_block.at[rows], out.at[rows], leave_send.at[part], leave_recv.at[part], across
        )

    attend(0)
    first_axis(0)
    attend(1)
    acc[:, :QCOLS] = jnp.zeros((TOK, QCOLS), jnp.float32)
    rows_on(0, 2)
    first_axis_far(0)
    first_axis(1)
    second_axis(0, 0, 2)
    rows_on(2, 4)
    second_axis(0, 2, 4)
    first_axis_far(1)
    second_axis_far(0)

    @pl.loop(0, SUB)
    def _(j):
        zo_copy(far, j, 1, 0, 2).wait_recv()
        pair_o_copy(far, j, 3).start()

    second_axis(1, 0, 1)
    pair_o_done(z, 0).wait_recv()
    pair_o_done(down, 1).wait_recv()
    pair_o_done(up, 2).wait_recv()
    pair_o_done(far, 3).wait_recv()
    combine(0, (0, 1))
    second_axis(1, 1, 2)
    combine(0, (3, 2))
    deliver(0)
    second_axis(1, 2, 4)
    combine(1, (0, 1, 3))
    second_axis_far(1)
    combine(1, (2,))
    deliver(1)

    @pl.when(owner)
    def _():
        for part in range(2):
            rows = pl.ds(START[part], SIZE[part])
            pltpu.make_async_copy(out_block.at[rows], out.at[rows], stay_sem.at[part]).wait()

    @pl.when(jnp.logical_not(owner))
    def _():
        for part in range(2):
            leave_copy(part).wait()

    def drained(ref, sem):
        remote(ref, ref, sem, kv_sem.at[1], partner).wait_send()

    drained(weights.at[0, pl.ds(0, 15), 0], a2a_send)
    for direction in range(2):
        drained(weights.at[0, pl.ds(0, 12)], z_send.at[direction])
        drained(weights_o.at[pl.ds(0, 3), 0, :, pl.ds(0, 2 * PIECE)], zo_send.at[direction])
    drained(weights.at[:, :, 0], pair_send)
    drained(weights_o.at[:, 0], pair_o_send)
    drained(kv.at[0], kv_sem.at[0])
    drained(ctx.at[pl.ds(0, 15)], ctx_send)

    @pl.when(owner)
    def _():
        drained(hid.at[pl.ds(0, SUB_ROWS), pl.ds(0, 7 * PIECE // 2)], cross_send)
        drained(seg, seg_sem.at[0])

    @pl.when(jnp.logical_not(owner))
    def _():
        drained(hid.at[pl.ds(0, SUB_ROWS), pl.ds(0, 7 * PIECE // 2)], inner_send)
        drained(hid.at[pl.ds(0, 3 * SUB_ROWS), pl.ds(0, 3 * PIECE)], ring_send)
        drained(send_o, swap_sem.at[0])


def tables():
    half = HEAD // 2
    freq = np.float32(rope_base) ** (
        np.float32(-2.0) * np.arange(half, dtype=np.float32) / np.float32(HEAD)
    )
    angle = np.arange(TOK, dtype=np.float32)[:, None] * freq.astype(np.float32)[None, :]
    cosine, sine = np.cos(angle), np.sin(angle)
    return (
        np.concatenate([cosine, cosine], axis=1).astype(np.float32),
        np.concatenate([-sine, sine], axis=1).astype(np.float32),
    )


def shards(ckpt_query, ckpt_key, ckpt_value, ckpt_output, hidden_in, segment_ids):
    bf16, f32 = jnp.bfloat16, jnp.float32
    dma = pltpu.SemaphoreType.DMA
    cosine, sine = tables()
    anywhere = pl.BlockSpec(memory_space=pl.ANY)
    return pl.pallas_call(
        kernel,
        out_shape=jax.ShapeDtypeStruct((TOK, TOK), bf16),
        in_specs=[anywhere] * 8,
        out_specs=anywhere,
        scratch_shapes=[
            pltpu.VMEM((16, 4, ROWS, QCOLS), bf16),
            pltpu.VMEM((2, 4, ROWS, 1024), bf16),
            pltpu.VMEM((4, ROWS, D), bf16),
            pltpu.VMEM((2, 8, ROWS, HEAD), bf16),
            pltpu.VMEM((16, ROWS, WCOLS), bf16),
            pltpu.VMEM((ROWS, D), bf16),
            pltpu.VMEM((4, 16, 2, ROWS, WCOLS), bf16),
            pltpu.VMEM((TOK, D), bf16),
            pltpu.VMEM((TOK, WCOLS), f32),
            pltpu.VMEM((4, 2, ROWS, D), bf16),
            pltpu.VMEM((16, HEADS_CHIP, TOK, HEAD), bf16),
            pltpu.VMEM((HEADS_CHIP, TOK, HEAD), bf16),
            pltpu.VMEM((2, TOK, HEAD), bf16),
            pltpu.VMEM((1, TOK), jnp.int32),
            pltpu.VMEM((2, TOK, HEAD), f32),
            pltpu.VMEM((TOK, TOK), bf16),
            dma((16,)),
            dma((5,)),
            dma,
            dma((16,)),
            dma((2,)),
            dma((3, 16)),
            dma,
            dma((4,)),
            dma((2,)),
            dma,
            dma((5,)),
            dma,
            dma((5,)),
            dma,
            dma((3, 2, 3)),
            dma((2,)),
            dma((2,)),
            dma((2,)),
            dma((2,)),
            dma((3, SUB)),
            dma,
            dma((4,)),
            dma,
            dma((2, 16, HEADS_CHIP)),
            dma((2,)),
            dma((2,)),
            dma((2,)),
        ],
        compiler_params=pltpu.CompilerParams(
            collective_id=0, has_side_effects=True, vmem_limit_bytes=66_000_000
        ),
    )(ckpt_query, ckpt_key, ckpt_value, ckpt_output, hidden_in, segment_ids, cosine, sine)


def solution(mesh):
    placed = (
        P(None, ("dp", "head"), None),
        P(None, ("dp", "head"), None),
        P(None, ("dp", "head"), None),
        P(None, ("head", "dp"), None),
        P("dp", None),
        P("dp", None),
    )
    return jax.shard_map(
        shards, mesh=mesh, in_specs=placed, out_specs=P("dp", "head"), check_vma=False
    )
```

```python
import functools

import jax
import jax.numpy as jnp
import numpy as np
from jax import lax
from jax.experimental import pallas as pl
from jax.experimental.pallas import tpu as pltpu
from jax.sharding import PartitionSpec as P

MESH = pl.DeviceIdType.MESH
rope_base = 500000.0
N = 4
TOK = 512
HEAD = 128
HEADS_CHIP = 4
QCOLS = HEADS_CHIP * HEAD
WCOLS = QCOLS + HEAD
ROWS = 64
D = 8192
SUB = 4
PIECE = D // N
SUB_ROWS = TOK // 4
START = (0, 128)
SIZE = (128, 384)


def average(stack):
    return (jnp.sum(stack.astype(jnp.float32), axis=0) * 0.25).astype(jnp.bfloat16)


def wrap(value):
    return lax.rem(value, N)


def device(x, y, z, c):
    return (2 * z + lax.div(y, 2), 8 * lax.rem(y, 2) + 2 * x + c)


def kernel(
    ckpt_q, ckpt_k, ckpt_v, ckpt_o, hidden, segments, cosine, sine, out,
    stage_q, stage_kv, stage_o, mean_kv, send_w, send_o, weights, hid, acc, weights_o,
    ctx, q_rot, kv, seg, table, out_block,
    stage_q_sem, stage_sem, a2a_send, a2a_recv, z_send, z_recv, pair_send, pair_recv,
    hid_sem, cross_send, cross_recv, inner_send, inner_recv, ring_send, ring_recv, kv_sem, seg_sem,
    swap_sem, zo_send, zo_recv, pair_o_send, pair_o_recv, ctx_send, ctx_recv,
    stay_sem, leave_send, leave_recv,
):
    dp = lax.axis_index("dp")
    head = lax.axis_index("head")
    z = lax.div(dp, 2)
    y_hi = lax.rem(dp, 2)
    y = 2 * y_hi + lax.div(head, 8)
    x = wrap(lax.div(head, 2))
    c = lax.rem(head, 2)
    place = 4 * y + x
    owner = c == y_hi
    up, down, far = wrap(z + 1), wrap(z + 3), wrap(z + 2)
    here_up, here_down = device(x, y, up, c), device(x, y, down, c)
    partner = device(x, y, z, 1 - c)
    across = device(x, wrap(y + 2), z, 1 - c)
    cross = device(x, 3 - y, z, c)

    def remote(src, dst, send, recv, where):
        return pltpu.make_async_remote_copy(
            src_ref=src, dst_ref=dst, send_sem=send, recv_sem=recv,
            device_id=where, device_id_type=MESH,
        )

    def spot(k):
        dx, dy = lax.rem(k, N), lax.div(k, N)
        tx, ty = wrap(x + dx), wrap(y + dy)
        fx, fy = wrap(x + N - dx), wrap(y + N - dy)
        return tx, ty, 4 * ty + tx, 4 * fy + fx

    def stage_copy(k):
        _, _, to, _ = spot(k)
        return pltpu.make_async_copy(
            ckpt_q.at[:, :, pl.ds(pl.multiple_of(to * QCOLS, QCOLS), QCOLS)],
            stage_q.at[k], stage_q_sem.at[k],
        )

    load_k = pltpu.make_async_copy(ckpt_k, stage_kv.at[0], stage_sem.at[0])
    load_v = pltpu.make_async_copy(ckpt_v, stage_kv.at[1], stage_sem.at[1])
    load_o = pltpu.make_async_copy(ckpt_o, stage_o, stage_sem.at[2])
    load_cos = pltpu.make_async_copy(cosine, table.at[0], stage_sem.at[3])
    load_sin = pltpu.make_async_copy(sine, table.at[1], stage_sem.at[4])
    load_k.start()
    load_v.start()

    @pl.loop(0, 16)
    def _(k):
        stage_copy(k).start()

    load_o.start()
    load_cos.start()
    load_sin.start()

    barrier = pltpu.get_barrier_semaphore()

    @pl.loop(1, 16)
    def _(k):
        tx, ty, _, _ = spot(k)
        pl.semaphore_signal(barrier, inc=1, device_id=device(tx, ty, z, c), device_id_type=MESH)

    for peer in (here_up, here_down, partner, across):
        pl.semaphore_signal(barrier, inc=1, device_id=peer, device_id_type=MESH)

    load_k.wait()
    load_v.wait()
    for which in range(2):
        for g in range(8):
            mean_kv[which, g] = average(stage_kv[which, :, :, g * HEAD : (g + 1) * HEAD])

    pl.semaphore_wait(barrier, 19)

    def a2a_copy(k):
        tx, ty, _, _ = spot(k)
        return remote(
            send_w.at[k], weights.at[z, place, c], a2a_send, a2a_recv.at[k], device(tx, ty, z, c)
        )

    def piece(k):
        _, _, to, _ = spot(k)
        stage_copy(k).wait()
        return average(stage_q[k]), mean_kv[lax.rem(to, 2), lax.div(to, 2)]

    side = lax.rem(y, 2)
    inner = device(x, y + 1 - 2 * side, z, c)
    east, west, far_x = wrap(x + 1), wrap(x + 3), wrap(x + 2)

    def strip(ref, at_x, eighth, j):
        start = pl.multiple_of(at_x * PIECE + eighth * (PIECE // 2), PIECE // 2)
        return ref.at[pl.ds((j + 1) * SUB_ROWS, SUB_ROWS), pl.ds(start, PIECE // 2)]

    def top(ref, half, i):
        start = pl.multiple_of((2 * half + i) * PIECE, PIECE)
        return ref.at[pl.ds(0, SUB_ROWS), pl.ds(start, PIECE)]

    def cross_copy(j):
        return remote(
            strip(hidden, x, side, j), strip(hid, x, side, j), cross_send, cross_recv.at[j], cross
        )

    def cross_top(i):
        return remote(
            top(hidden, side, i), top(hid, side, i), cross_send, cross_recv.at[3 + i], cross
        )

    def cross_wait(j):
        block = strip(hid, x, 1 - side, j)
        remote(block, block, cross_send, cross_recv.at[j], cross).wait_recv()

    def inner_copy(j):
        block = strip(hid, x, 1 - side, j)
        return remote(block, block, inner_send, inner_recv.at[j], inner)

    def inner_wait(j):
        block = strip(hid, x, side, j)
        remote(block, block, inner_send, inner_recv.at[j], inner).wait_recv()

    def ring_copy(at_x, eighth, j, direction, slot):
        block = strip(hid, at_x, eighth, j)
        return remote(
            block, block, ring_send, ring_recv.at[slot, eighth, j],
            device(wrap(x + direction), y, z, c),
        )

    def event(number):
        if number < 3:
            cross_wait(number)
            inner_copy(number).start()
            ring_copy(x, 1 - side, number, 1, 0).start()
            ring_copy(x, 1 - side, number, 3, 1).start()
        if 1 <= number < 4:
            inner_wait(number - 1)
            ring_copy(x, side, number - 1, 1, 0).start()
            ring_copy(x, side, number - 1, 3, 1).start()
        if 3 <= number < 5:
            block = top(hid, 1 - side, number - 3)
            remote(block, block, cross_send, cross_recv.at[number], cross).wait_recv()
            remote(block, block, inner_send, inner_recv.at[number], inner).start()
        if 5 <= number < 8:
            j = number - 5

            def far_on(eighth):
                ring_copy(west, eighth, j, 1, 0).wait_recv()
                ring_copy(east, eighth, j, 3, 1).wait_recv()

            far_on(1 - side)
            far_on(side)
            ring_copy(west, 0, j, 1, 2).start()
            ring_copy(east, 1, j, 3, 2).start()

    def events(*numbers):
        @pl.when(jnp.logical_not(owner))
        def _():
            for number in numbers:
                event(number)

    def seg_copy():
        return remote(segments, seg, seg_sem.at[0], seg_sem.at[1], cross)

    local_hid = pltpu.make_async_copy(hidden, hid, hid_sem.at[0])
    local_seg = pltpu.make_async_copy(segments, seg, hid_sem.at[1])

    first_q, first_kv = piece(0)
    weights[z, place, c, :, :QCOLS] = first_q
    weights[z, place, c, :, QCOLS:] = first_kv

    @pl.loop(1, 16)
    def _(k):
        mean_q, mean_pair = piece(k)
        send_w[k, :, :QCOLS] = mean_q
        send_w[k, :, QCOLS:] = mean_pair

        @pl.when(k > 1)
        def _():
            a2a_copy(k - 1).start()

        @pl.when(owner & (lax.rem(k, 5) == 4))
        def _():
            cross_copy(lax.div(k, 5)).start()

    a2a_copy(15).start()

    @pl.when(owner)
    def _():
        cross_top(0).start()
        cross_top(1).start()
        seg_copy().start()
        local_hid.start()
        local_seg.start()

    def z_copy(level, k, direction, send_index, recv_index):
        _, _, _, source = spot(k)
        block = weights.at[level, source, c]
        return remote(
            block, block, z_send.at[send_index], z_recv.at[recv_index, k],
            here_up if direction > 0 else here_down,
        )

    def pair_copy(level, k, slot):
        _, _, _, source = spot(k)
        block = weights.at[level, source, c]
        return remote(block, block, pair_send, pair_recv.at[slot], partner)

    def pair_done(level, slot):
        block = weights.at[level, :, 1 - c]
        return remote(block, block, pair_send, pair_recv.at[slot], partner)

    def a2a_arrival(k):
        _, _, _, source = spot(k)
        block = weights.at[z, source, c]
        return remote(block, block, a2a_send, a2a_recv.at[k], partner)

    def own_part(lo, hi):
        @pl.loop(lo, hi)
        def _(k):
            @pl.when(k > 0)
            def _():
                a2a_arrival(k).wait_recv()

            z_copy(z, k, 1, 0, 0).start()
            z_copy(z, k, -1, 1, 1).start()
            pair_copy(z, k, 0).start()

    own_part(0, 8)

    load_o.wait()
    step = D // 8

    @pl.when(owner)
    def _():
        @pl.loop(0, 8)
        def _(j):
            cols = pl.ds(pl.multiple_of(j * step, step), step)
            weights_o[z, c, :, cols] = average(stage_o[:, :, cols])

    def swap_copy():
        return remote(
            send_o, weights_o.at[z, y_hi], swap_sem.at[0], swap_sem.at[1], across
        )

    @pl.when(jnp.logical_not(owner))
    def _():
        @pl.loop(0, 8)
        def _(j):
            cols = pl.ds(pl.multiple_of(j * step, step), step)
            send_o[:, cols] = average(stage_o[:, :, cols])

    events(0)
    own_part(8, 12)
    events(1)
    own_part(12, 16)
    events(2, 3)

    def pass_on(lo, hi):
        @pl.loop(lo, hi)
        def _(k):
            z_copy(down, k, 1, 0, 0).wait_recv()

            @pl.when(lax.rem(k, 2) == 0)
            def _():
                z_copy(down, k, 1, 0, 2).start()

            pair_copy(down, k, 1).start()
            z_copy(up, k, -1, 1, 1).wait_recv()

            @pl.when(lax.rem(k, 2) == 1)
            def _():
                z_copy(up, k, -1, 1, 2).start()

            pair_copy(up, k, 2).start()

    pass_on(0, 4)
    events(4)
    pass_on(4, 8)
    events(5)
    pass_on(8, 12)
    events(6)
    pass_on(12, 16)
    events(7)

    def o_block(level, core, j):
        return weights_o.at[level, core, :, pl.ds(pl.multiple_of(j * PIECE, PIECE), PIECE)]

    def zo_copy(level, j, direction, send_index, recv_index):
        block = o_block(level, c, j)
        return remote(
            block, block, zo_send.at[send_index], zo_recv.at[recv_index, j],
            here_up if direction > 0 else here_down,
        )

    def pair_o_copy(level, j, slot):
        block = o_block(level, c, j)
        return remote(block, block, pair_o_send, pair_o_recv.at[slot], partner)

    def pair_o_done(level, slot):
        block = weights_o.at[level, 1 - c]
        return remote(block, block, pair_o_send, pair_o_recv.at[slot], partner)

    @pl.when(owner)
    def _():
        local_hid.wait()
        local_seg.wait()

    @pl.when(jnp.logical_not(owner))
    def _():
        swap_copy().start()
        for i in range(2):
            block = top(hid, side, i)
            remote(block, block, inner_send, inner_recv.at[3 + i], inner).wait_recv()

        @pl.loop(0, 3)
        def _(j):
            ring_copy(far_x, 0, j, 1, 2).wait_recv()
            ring_copy(far_x, 1, j, 1, 2).wait_recv()

        seg_copy().wait_recv()

    load_cos.wait()
    load_sin.wait()
    acc[...] = jnp.zeros_like(acc)

    def project(level, lo, hi):
        block = weights[level, :, :, :, lo:hi].reshape(PIECE, hi - lo)
        rows = hid[:, pl.ds(pl.multiple_of(level * PIECE, PIECE), PIECE)]
        acc[:, lo:hi] += jnp.dot(rows, block, preferred_element_type=jnp.float32)

    def rotate(values, rows=slice(None)):
        return values * table[0, rows] + pltpu.roll(values, HEAD // 2, 1) * table[1, rows]

    parity = lax.rem(x, 2)
    kv_peer = device(x + 1 - 2 * parity, y, z, c)
    kv_out = remote(kv.at[parity], kv.at[parity], kv_sem.at[0], kv_sem.at[1], kv_peer)
    kv_in = remote(kv.at[1 - parity], kv.at[1 - parity], kv_sem.at[0], kv_sem.at[1], kv_peer)

    @pl.loop(0, 4)
    def _(i):
        level = wrap(z + jnp.where(i == 1, 3, jnp.where(i == 2, 1, jnp.where(i == 3, 2, 0))))

        @pl.loop(0, 4)
        def _(inner_k):
            k = 4 * i + inner_k
            z_copy(far, k, 1, 0, 2).wait_recv()
            pair_copy(far, k, 3).start()

        @pl.when(i == 3)
        def _():
            @pl.when(jnp.logical_not(owner))
            def _():
                block = weights_o.at[z, c]
                remote(block, block, swap_sem.at[0], swap_sem.at[1], across).wait_recv()

            @pl.loop(0, SUB)
            def _(j):
                zo_copy(z, j, 1, 0, 0).start()
                zo_copy(z, j, -1, 1, 1).start()
                pair_o_copy(z, j, 0).start()

        pair_done(level, i).wait_recv()
        project(level, QCOLS, WCOLS)

        @pl.when(i == 3)
        def _():
            mine = acc[:, QCOLS:]
            kv[parity] = jnp.where(parity == 0, rotate(mine), mine).astype(jnp.bfloat16)
            kv_out.start()

        project(level, 0, QCOLS)

    for h in range(HEADS_CHIP):
        q_rot[h] = rotate(acc[:, h * HEAD : (h + 1) * HEAD]).astype(jnp.bfloat16)
    kv_in.wait_recv()

    segment_row = seg[...].astype(jnp.float32)
    segment_col = jnp.transpose(jnp.broadcast_to(segment_row, (HEAD, TOK)))[:, :1]

    def ctx_copy(part, place_from, h, where, slot):
        block = ctx.at[place_from, h, pl.ds(START[part], SIZE[part])]
        return remote(block, block, ctx_send, ctx_recv.at[part, slot, h], where)

    def line(h, along, by):
        on_x = lax.rem(lax.div(h, 2) + along, 2) == 0
        step_x = jnp.where(on_x, by, 0)
        step_y = jnp.where(on_x, 0, by)
        return device(wrap(x + step_x), wrap(y + step_y), z, c)

    def block_at(h, first, second):
        on_x = lax.div(h, 2) == 0
        step_x = jnp.where(on_x, first, second)
        step_y = jnp.where(on_x, second, first)
        return 4 * wrap(y + step_y) + wrap(x + step_x)

    def attend(part):
        width = START[part] + SIZE[part]
        rows = slice(START[part], width)
        row_at = lax.broadcasted_iota(jnp.int32, (SIZE[part], width), 0) + START[part]
        col_at = lax.broadcasted_iota(jnp.int32, (SIZE[part], width), 1)
        allowed = (row_at >= col_at) & (segment_col[rows] == segment_row[:, :width])

        @pl.loop(0, HEADS_CHIP)
        def _(h):
            scores = lax.dot_general(
                q_rot[h, rows], kv[0, :width], (((1,), (1,)), ((), ())),
                preferred_element_type=jnp.float32,
            ) * HEAD ** (-0.5)
            scores = jnp.where(allowed, scores, -1e30)
            peak = jnp.max(scores, axis=-1, keepdims=True)
            raised = jnp.exp(scores - peak)
            probs = (raised * (1.0 / jnp.sum(raised, axis=-1, keepdims=True))).astype(jnp.bfloat16)
            ctx[place, h, rows] = jnp.dot(
                probs, kv[1, :width], preferred_element_type=jnp.float32
            ).astype(jnp.bfloat16)
            ctx_copy(part, place, h, line(h, 0, 1), 1).start()
            ctx_copy(part, place, h, line(h, 0, 3), 3).start()
            ctx_copy(part, place, h, line(h, 1, 1), 4).start()
            ctx_copy(part, place, h, line(h, 1, 3), 12).start()

    def ctx_wait(part, h, first, second, slot):
        block = ctx.at[block_at(h, first, second), h, pl.ds(START[part], SIZE[part])]
        remote(block, block, ctx_send, ctx_recv.at[part, slot, h], partner).wait_recv()

    def onward(part, h, slot):
        source = block_at(h, 4 - slot, 0)

        @pl.when(lax.rem(h, 2) == (0 if slot == 1 else 1))
        def _():
            ctx_copy(part, source, h, line(h, 0, slot), 2).start()

        ctx_copy(part, source, h, line(h, 1, 1), 4 + slot).start()
        ctx_copy(part, source, h, line(h, 1, 3), 12 + slot).start()

    def first_axis(part):
        @pl.loop(0, HEADS_CHIP)
        def _(h):
            ctx_wait(part, h, 3, 0, 1)
            onward(part, h, 1)
            ctx_wait(part, h, 1, 0, 3)
            onward(part, h, 3)

    def first_axis_far(part):
        @pl.loop(0, HEADS_CHIP)
        def _(h):
            ctx_wait(part, h, 2, 0, 2)
            source = block_at(h, 2, 0)
            ctx_copy(part, source, h, line(h, 1, 1), 4 + 2).start()
            ctx_copy(part, source, h, line(h, 1, 3), 12 + 2).start()

    def second_axis(part, lo, hi):
        @pl.loop(lo, hi)
        def _(i):
            t = jnp.where(i == 2, 3, jnp.where(i == 3, 2, i))
            first = wrap(N - t)

            @pl.loop(0, HEADS_CHIP)
            def _(h):
                even = lax.rem(h, 2) == 0
                ctx_wait(part, h, first, 3, 4 + t)

                @pl.when(even)
                def _():
                    ctx_copy(part, block_at(h, first, 3), h, line(h, 1, 1), 8 + t).start()

                ctx_wait(part, h, first, 1, 12 + t)

                @pl.when(jnp.logical_not(even))
                def _():
                    ctx_copy(part, block_at(h, first, 1), h, line(h, 1, 3), 8 + t).start()

    def second_axis_far(part):
        @pl.loop(0, 4)
        def _(t):
            @pl.loop(0, HEADS_CHIP)
            def _(h):
                ctx_wait(part, h, wrap(N - t), 2, 8 + t)

    def rows_on(lo, hi):
        @pl.loop(lo, hi)
        def _(j):
            zo_copy(down, j, 1, 0, 0).wait_recv()

            @pl.when(lax.rem(j, 2) == 0)
            def _():
                zo_copy(down, j, 1, 0, 2).start()

            pair_o_copy(down, j, 1).start()
            zo_copy(up, j, -1, 1, 1).wait_recv()

            @pl.when(lax.rem(j, 2) == 1)
            def _():
                zo_copy(up, j, -1, 1, 2).start()

            pair_o_copy(up, j, 2).start()

    def combine(part, offsets):
        rows = pl.ds(START[part], SIZE[part])

        @pl.loop(0, len(offsets))
        def _(i):
            offset = offsets[0]
            for at in range(1, len(offsets)):
                offset = jnp.where(i == at, offsets[at], offset)
            places = [(4 * wrap(y + offset) + along, 0) for along in range(N)]
            places += [(4 * along + wrap(x + offset), 2) for along in range(N)]
            left = jnp.concatenate(
                [ctx[p, first + h, rows] for p, first in places for h in range(2)], axis=1
            )
            right = jnp.concatenate(
                [
                    weights_o[
                        :, :, :,
                        pl.ds(pl.multiple_of(p * QCOLS + first * HEAD, 2 * HEAD), 2 * HEAD),
                    ].reshape(TOK, 2 * HEAD)
                    for p, first in places
                ],
                axis=1,
            )
            acc[rows, :QCOLS] += lax.dot_general(
                left, right, (((1,), (1,)), ((), ())), preferred_element_type=jnp.float32
            )

    def deliver(part):
        rows = pl.ds(START[part], SIZE[part])
        out_block[rows] = acc[rows, :QCOLS].astype(jnp.bfloat16)

        @pl.when(owner)
        def _():
            pltpu.make_async_copy(out_block.at[rows], out.at[rows], stay_sem.at[part]).start()

        @pl.when(jnp.logical_not(owner))
        def _():
            leave_copy(part).start()

    def leave_copy(part):
        rows = pl.ds(START[part], SIZE[part])
        return remote(
            out_block.at[rows], out.at[rows], leave_send.at[part], leave_recv.at[part], across
        )

    attend(0)
    first_axis(0)
    attend(1)
    acc[:, :QCOLS] = jnp.zeros((TOK, QCOLS), jnp.float32)
    rows_on(0, 2)
    first_axis_far(0)
    first_axis(1)
    second_axis(0, 0, 2)
    rows_on(2, 4)
    second_axis(0, 2, 4)
    first_axis_far(1)
    second_axis_far(0)

    @pl.loop(0, SUB)
    def _(j):
        zo_copy(far, j, 1, 0, 2).wait_recv()
        pair_o_copy(far, j, 3).start()

    second_axis(1, 0, 1)
    pair_o_done(z, 0).wait_recv()
    pair_o_done(down, 1).wait_recv()
    pair_o_done(up, 2).wait_recv()
    pair_o_done(far, 3).wait_recv()
    combine(0, (0, 1))
    second_axis(1, 1, 2)
    combine(0, (3, 2))
    deliver(0)
    second_axis(1, 2, 4)
    combine(1, (0, 1, 3))
    second_axis_far(1)
    combine(1, (2,))
    deliver(1)

    @pl.when(owner)
    def _():
        for part in range(2):
            rows = pl.ds(START[part], SIZE[part])
            pltpu.make_async_copy(out_block.at[rows], out.at[rows], stay_sem.at[part]).wait()

    @pl.when(jnp.logical_not(owner))
    def _():
        for part in range(2):
            leave_copy(part).wait()

    def drained(ref, sem):
        remote(ref, ref, sem, kv_sem.at[1], partner).wait_send()

    drained(weights.at[0, pl.ds(0, 15), 0], a2a_send)
    for direction in range(2):
        drained(weights.at[0, pl.ds(0, 12)], z_send.at[direction])
        drained(weights_o.at[pl.ds(0, 3), 0, :, pl.ds(0, 2 * PIECE)], zo_send.at[direction])
    drained(weights.at[:, :, 0], pair_send)
    drained(weights_o.at[:, 0], pair_o_send)
    drained(kv.at[0], kv_sem.at[0])
    drained(ctx.at[pl.ds(0, 15)], ctx_send)

    @pl.when(owner)
    def _():
        drained(hid.at[pl.ds(0, SUB_ROWS), pl.ds(0, 7 * PIECE // 2)], cross_send)
        drained(seg, seg_sem.at[0])

    @pl.when(jnp.logical_not(owner))
    def _():
        drained(hid.at[pl.ds(0, SUB_ROWS), pl.ds(0, 7 * PIECE // 2)], inner_send)
        drained(hid.at[pl.ds(0, 3 * SUB_ROWS), pl.ds(0, 3 * PIECE)], ring_send)
        drained(send_o, swap_sem.at[0])


def tables():
    half = HEAD // 2
    freq = np.float32(rope_base) ** (
        np.float32(-2.0) * np.arange(half, dtype=np.float32) / np.float32(HEAD)
    )
    angle = np.arange(TOK, dtype=np.float32)[:, None] * freq.astype(np.float32)[None, :]
    cosine, sine = np.cos(angle), np.sin(angle)
    return (
        np.concatenate([cosine, cosine], axis=1).astype(np.float32),
        np.concatenate([-sine, sine], axis=1).astype(np.float32),
    )


def shards(ckpt_query, ckpt_key, ckpt_value, ckpt_output, hidden_in, segment_ids):
    bf16, f32 = jnp.bfloat16, jnp.float32
    dma = pltpu.SemaphoreType.DMA
    cosine, sine = tables()
    anywhere = pl.BlockSpec(memory_space=pl.ANY)
    return pl.pallas_call(
        kernel,
        out_shape=jax.ShapeDtypeStruct((TOK, TOK), bf16),
        in_specs=[anywhere] * 8,
        out_specs=anywhere,
        scratch_shapes=[
            pltpu.VMEM((16, 4, ROWS, QCOLS), bf16),
            pltpu.VMEM((2, 4, ROWS, 1024), bf16),
            pltpu.VMEM((4, ROWS, D), bf16),
            pltpu.VMEM((2, 8, ROWS, HEAD), bf16),
            pltpu.VMEM((16, ROWS, WCOLS), bf16),
            pltpu.VMEM((ROWS, D), bf16),
            pltpu.VMEM((4, 16, 2, ROWS, WCOLS), bf16),
            pltpu.VMEM((TOK, D), bf16),
            pltpu.VMEM((TOK, WCOLS), f32),
            pltpu.VMEM((4, 2, ROWS, D), bf16),
            pltpu.VMEM((16, HEADS_CHIP, TOK, HEAD), bf16),
            pltpu.VMEM((HEADS_CHIP, TOK, HEAD), bf16),
            pltpu.VMEM((2, TOK, HEAD), bf16),
            pltpu.VMEM((1, TOK), jnp.int32),
            pltpu.VMEM((2, TOK, HEAD), f32),
            pltpu.VMEM((TOK, TOK), bf16),
            dma((16,)),
            dma((5,)),
            dma,
            dma((16,)),
            dma((2,)),
            dma((3, 16)),
            dma,
            dma((4,)),
            dma((2,)),
            dma,
            dma((5,)),
            dma,
            dma((5,)),
            dma,
            dma((3, 2, 3)),
            dma((2,)),
            dma((2,)),
            dma((2,)),
            dma((2,)),
            dma((3, SUB)),
            dma,
            dma((4,)),
            dma,
            dma((2, 16, HEADS_CHIP)),
            dma((2,)),
            dma((2,)),
            dma((2,)),
        ],
        compiler_params=pltpu.CompilerParams(
            collective_id=0, has_side_effects=True, vmem_limit_bytes=66_000_000
        ),
    )(ckpt_query, ckpt_key, ckpt_value, ckpt_output, hidden_in, segment_ids, cosine, sine)


def solution(mesh):
    placed = (
        P(None, ("dp", "head"), None),
        P(None, ("dp", "head"), None),
        P(None, ("dp", "head"), None),
        P(None, ("head", "dp"), None),
        P("dp", None),
        P("dp", None),
    )
    return jax.shard_map(
        shards, mesh=mesh, in_specs=placed, out_specs=P("dp", "head"), check_vma=False
    )
```
